256 devices in a mesh: vocab: 8 (over x_lo, y), ctx: 32 (over z, x_hi, core).
Axes of the slice: x: 4 (x_hi: 2, x_lo: 2; x = x_hi * 2 + x_lo), y: 4, z: 8, core: 2. Of those that a mesh axis runs over, the one named last changes fastest.
Arguments:
- hidden: bfloat16 [4096, 8192], P('ctx', 'vocab'), may hold values from -20 to 20
- norm_gain: float32 [8192], replicated, may hold values from 0.5 to 1.5
- head_weight: bfloat16 [152064, 8192], P(('vocab', 'ctx')), may hold values from -16 to 16
- targets: int32 [256], replicated, may hold values from 0 to 152063
- loss_rows: int32 [256], replicated, may hold values from 0 to 127, as said below
- stretch_of_slot: int32 [64], replicated, may hold values from 0 to 63, as said below
- queries: bfloat16 [4096, 8192], P('ctx', 'vocab'), may hold values from -20 to 20
- key_states: bfloat16 [4096, 1024], P('ctx', 'vocab'), may hold values from -20 to 20
- attention_values: bfloat16 [4096, 1024], P('ctx', 'vocab'), may hold values from -6 to 6
- output_weight: bfloat16 [8192, 8192], P('vocab', 'ctx'), may hold values from -0.0625 to 0.0625
Outputs:
- mean_loss: float32 [], replicated
- query_grad: bfloat16 [256, 8192], P('ctx', 'vocab')
- key_gradient: bfloat16 [4096, 1024], P('ctx', 'vocab')
- value_gradient: bfloat16 [4096, 1024], P('ctx', 'vocab')
- resid_grad: bfloat16 [8192, 256], P('ctx')
The draws below stay inside these ranges and needn't reach their ends.
Inputs may be any that keep to these rules, and one draw needn't show every extreme that they name: `loss_rows`: within each block of 8 entries, entry j lies in rows j * 16 to (j + 1) * 16 - 1. `stretch_of_slot`: A permutation of the stretches in which slots 2c and 2c+1 hold stretches that sum to 63.
All inputs are finite; a program needn't handle non-finite values.
Results may differ from the reference program's by a relative error of at most 0.023.
Values may be sent and summed in bfloat16 or wider, within the bound.
A program may use at most 64 MiB of HBM per device.

```python
import math
import jax
import jax.numpy as jnp
import numpy as np
from jax import lax

D = 8192
QUERY_HEAD_COUNT = 64
KEY_VALUE_HEADS = 8
HEAD_SIZE = 128
VOCAB = 152064
CH = 64
STRIDE = 16
T_DEV = 128
LPD = 8
STRETCHES = 64
SEQUENCE_TOKENS = 4096
LOSS = 256


def index_tables(key):
    half_count = STRETCHES // 2
    order_perm = jax.random.permutation(jax.random.fold_in(key, 101), half_count).astype(jnp.int32)
    flip_bits = jax.random.randint(jax.random.fold_in(key, 102), (half_count,), 0, 2).astype(jnp.int32)
    mirror = STRETCHES - 1 - order_perm
    leading = jnp.where(flip_bits == 1, mirror, order_perm)
    trailing = jnp.where(flip_bits == 1, order_perm, mirror)
    stretch_table = jnp.stack([leading, trailing], axis=1).reshape(STRETCHES).astype(jnp.int32)
    offsets = jax.random.randint(jax.random.fold_in(key, 103), (half_count, LPD), 0, STRIDE).astype(jnp.int32)
    offsets = offsets.at[0, 0].set(0).at[0, LPD - 1].set(STRIDE - 1)
    local_rows = offsets + STRIDE * jnp.arange(LPD, dtype=jnp.int32)[None, :]
    return (local_rows.reshape(LOSS).astype(jnp.int32), stretch_table)


def draw_loss_rows(key, part):
    return index_tables(key)[0]


def draw_stretch_of_slot(key, part):
    return index_tables(key)[1]


def hidden_field(key):
    normal_part = jnp.clip(jax.random.normal(jax.random.fold_in(key, 201), (SEQUENCE_TOKENS, D), jnp.float32), -6.0, 6.0)
    return normal_part.astype(jnp.bfloat16)


def draw_hidden(key, part):
    return hidden_field(key)


def draw_head_weight(key, part):
    weights = 3.0 * D ** (-0.5) * jnp.clip(jax.random.normal(jax.random.fold_in(key, 301), (VOCAB, D), jnp.float32), -6.0, 6.0)
    return weights.astype(jnp.bfloat16)


def draw_queries(key, part):
    value_rows_full = jnp.clip(jax.random.normal(jax.random.fold_in(key, 411), (SEQUENCE_TOKENS, QUERY_HEAD_COUNT * HEAD_SIZE), jnp.float32), -6.0, 6.0)
    return value_rows_full.astype(jnp.bfloat16)


def draw_key_states(key, part):
    value_rows_full = jnp.clip(jax.random.normal(jax.random.fold_in(key, 421), (SEQUENCE_TOKENS, KEY_VALUE_HEADS * HEAD_SIZE), jnp.float32), -6.0, 6.0)
    return value_rows_full.astype(jnp.bfloat16)


def set_ends(drawn, key, low, largest):
    extent = drawn.shape
    index_at = [jax.random.randint(jax.random.fold_in(key, axis), (), 0, extent[axis]) for axis in range(len(extent))]
    drawn = drawn.at[tuple(index_at)].set(low)
    longest = extent.index(max(extent))
    index_at[longest] = (index_at[longest] + 1) % extent[longest]
    return drawn.at[tuple(index_at)].set(largest)


def levels(own_key, extent, pieces, least, top_value):
    def one(dim, blocks):
        steps = jax.random.uniform(jax.random.fold_in(jax.random.fold_in(own_key, 6), dim), (blocks,), jnp.float32, least / len(pieces), top_value / len(pieces))
        return jnp.repeat(jnp.exp(steps), extent[dim] // blocks).reshape((-1,) + (1,) * (len(extent) - dim - 1))

    gain = one(*pieces[0])
    for cut in pieces[1:]:
        gain = gain * one(*cut)
    return gain


def wide_ids(stream_key, shape, amount, skew):
    weights = [min(1 << octave, amount + 1 - (1 << octave)) * (1 << 20) // math.isqrt((1 << octave) ** skew) + 1 for octave in range((amount + 1).bit_length()) if 1 << octave <= amount]
    deviation = 1 + sum(weights) // (1 << 30)
    listing = np.cumsum(np.array([max(1, weight // deviation) for weight in weights]))
    pick = jax.random.randint(jax.random.fold_in(stream_key, 1), shape, 0, int(listing[len(weights) - 1]))
    start = jnp.left_shift(1, jnp.searchsorted(jnp.asarray(listing, jnp.int32), pick, side="right").astype(jnp.int32))
    standing = start - 1 + jax.random.randint(jax.random.fold_in(stream_key, 4), shape, 0, 1 << 30) % jnp.minimum(start, amount + 1 - start)
    return jax.random.permutation(jax.random.fold_in(stream_key, 2), amount)[standing].astype(jnp.int32)


def normal_values(stream_key, extent, scale, most, split=(), kind=jnp.bfloat16):
    array = scale * jax.random.normal(stream_key, extent, jnp.float32)
    if split:
        array = array * levels(stream_key, extent, split, -0.22, 0.18)
    return jnp.clip(array, -most, most).astype(kind)


def setup_inputs(seed: int = 0) -> dict:
    keys = jax.random.split(jax.random.key(seed), 11)
    hidden = draw_hidden(jax.random.fold_in(keys[10], 71), 0)
    norm_gain = jnp.clip(1.0 + 0.1 * jax.random.normal(keys[1], (D,), jnp.float32), 0.5, 1.5)
    head_weight = draw_head_weight(jax.random.fold_in(keys[10], 71), 0)
    targets = set_ends(wide_ids(keys[3], (LOSS,), VOCAB, 2), jax.random.fold_in(keys[3], 3), 0, VOCAB - 1).astype(jnp.int32)
    loss_rows = draw_loss_rows(jax.random.fold_in(keys[10], 71), 0)
    stretch_of_slot = draw_stretch_of_slot(jax.random.fold_in(keys[10], 71), 0)
    queries = draw_queries(jax.random.fold_in(keys[10], 71), 0)
    key_states = draw_key_states(jax.random.fold_in(keys[10], 71), 0)
    attention_values = normal_values(keys[8], (SEQUENCE_TOKENS, KEY_VALUE_HEADS * HEAD_SIZE), 1.0, 6.0, ((0, 32), (1, 8)))
    output_weight = normal_values(keys[9], (QUERY_HEAD_COUNT * HEAD_SIZE, D), (QUERY_HEAD_COUNT * HEAD_SIZE) ** -0.5, 0.0625, ((0, 8), (1, 32)))
    return dict(hidden=hidden, norm_gain=norm_gain, head_weight=head_weight, targets=targets, loss_rows=loss_rows, stretch_of_slot=stretch_of_slot, queries=queries, key_states=key_states, attention_values=attention_values, output_weight=output_weight)


norm_eps = 1e-06
grad_weight = 16.0
masked_fill = -1e+30

def head_attention(query_heads, grad_heads, query_pos, key_heads, value_heads, key_pos):
    score_scale = HEAD_SIZE ** (-0.5)
    highest = lax.Precision.HIGHEST
    query_f = query_heads.astype(jnp.float32)
    grad_f = grad_heads.astype(jnp.float32)
    key_f = key_heads.astype(jnp.float32)
    value_f = value_heads.astype(jnp.float32)
    scores = jnp.einsum('tgd,sd->gts', query_f, key_f, precision=highest) * score_scale
    visible = key_pos[None, None, :] <= query_pos[None, :, None]
    masked = jnp.where(visible, scores, masked_fill)
    top_score = lax.optimization_barrier(jnp.max(masked, axis=2, keepdims=True))
    raw_weights = jnp.where(visible, jnp.exp(masked - top_score), 0.0)
    prob_full = raw_weights / lax.optimization_barrier(jnp.sum(raw_weights, axis=2, keepdims=True))
    output = jnp.einsum('gts,sd->gtd', prob_full, value_f, precision=highest)
    row_delta = lax.optimization_barrier(jnp.sum(output * jnp.transpose(grad_f, (1, 0, 2)), axis=2))
    prob_half = prob_full.astype(jnp.bfloat16).astype(jnp.float32)
    prob_grad = jnp.einsum('tgd,sd->gts', grad_f, value_f, precision=highest)
    score_grad = (prob_full * (prob_grad - row_delta[:, :, None])).astype(jnp.bfloat16).astype(jnp.float32)
    query_term = jnp.einsum('gts,sd->tgd', score_grad, key_f, precision=highest) * score_scale
    key_term = jnp.einsum('gts,tgd->sd', score_grad, query_f, precision=highest) * score_scale
    value_term = jnp.einsum('gts,tgd->sd', prob_half, grad_f, precision=highest)
    return (query_term, key_term, value_term)

def reference(hidden, norm_gain, head_weight, targets, loss_rows, stretch_of_slot, queries, key_states, attention_values, output_weight):
    owner_dev = jnp.arange(LOSS, dtype=jnp.int32) // LPD
    row_ids = (owner_dev * T_DEV + loss_rows).astype(jnp.int32)
    picked = hidden[row_ids].astype(jnp.float32)
    inv_rms = lax.rsqrt(lax.optimization_barrier(jnp.mean(picked * picked, axis=1)) + norm_eps)
    normed = (picked * inv_rms[:, None] * norm_gain[None, :]).astype(jnp.bfloat16)
    logits = jnp.dot(normed, head_weight.T, preferred_element_type=jnp.float32)
    top_score = lax.optimization_barrier(jnp.max(logits, axis=1))
    row_total = lax.optimization_barrier(jnp.sum(jnp.exp(logits - top_score[:, None]), axis=1))
    log_total = top_score + jnp.log(row_total)
    vocab_ids = jnp.arange(VOCAB, dtype=jnp.int32)
    is_target = vocab_ids[None, :] == targets[:, None]
    target_logit = lax.optimization_barrier(jnp.sum(jnp.where(is_target, logits, 0.0), axis=1))
    mean_loss = jnp.mean(log_total - target_logit)
    logit_grad = (grad_weight * (jnp.exp(logits - log_total[:, None]) - is_target.astype(jnp.float32))).astype(jnp.bfloat16)
    normed_grad = jnp.dot(logit_grad, head_weight, preferred_element_type=jnp.float32)
    scaled = normed_grad * norm_gain[None, :]
    unit_rows = picked * inv_rms[:, None]
    inner = lax.optimization_barrier(jnp.sum(scaled * unit_rows, axis=1)) / D
    resid_grad = (inv_rms[:, None] * (scaled - unit_rows * inner[:, None])).astype(jnp.bfloat16)
    attn_grad = jnp.dot(resid_grad, output_weight.T, preferred_element_type=jnp.float32).astype(jnp.bfloat16)
    slot_ids = jnp.arange(SEQUENCE_TOKENS, dtype=jnp.int32)
    key_pos = (stretch_of_slot[slot_ids // CH] * CH + slot_ids % CH).astype(jnp.int32)
    query_pos = key_pos[row_ids]
    query_loss = queries[row_ids]
    query_group_size = QUERY_HEAD_COUNT // KEY_VALUE_HEADS

    def each_head_rows(head_index):
        start = (head_index * query_group_size * HEAD_SIZE).astype(jnp.int32)
        query_heads = lax.dynamic_slice_in_dim(query_loss, start, query_group_size * HEAD_SIZE, 1).reshape(LOSS, query_group_size, HEAD_SIZE)
        grad_heads = lax.dynamic_slice_in_dim(attn_grad, start, query_group_size * HEAD_SIZE, 1).reshape(LOSS, query_group_size, HEAD_SIZE)
        key_start = (head_index * HEAD_SIZE).astype(jnp.int32)
        key_heads = lax.dynamic_slice_in_dim(key_states, key_start, HEAD_SIZE, 1)
        value_heads = lax.dynamic_slice_in_dim(attention_values, key_start, HEAD_SIZE, 1)
        return head_attention(query_heads, grad_heads, query_pos, key_heads, value_heads, key_pos)
    gathered_queries, gathered_keys, gathered_values = lax.map(each_head_rows, jnp.arange(KEY_VALUE_HEADS, dtype=jnp.int32))
    query_grad = jnp.transpose(gathered_queries, (1, 0, 2, 3)).reshape(LOSS, QUERY_HEAD_COUNT * HEAD_SIZE).astype(jnp.bfloat16)
    key_gradient = jnp.transpose(gathered_keys, (1, 0, 2)).reshape(SEQUENCE_TOKENS, KEY_VALUE_HEADS * HEAD_SIZE).astype(jnp.bfloat16)
    value_gradient = jnp.transpose(gathered_values, (1, 0, 2)).reshape(SEQUENCE_TOKENS, KEY_VALUE_HEADS * HEAD_SIZE).astype(jnp.bfloat16)
    return (mean_loss, query_grad, key_gradient, value_gradient, resid_grad.T)
```

```python
import functools

import jax
import jax.numpy as jnp
from jax import lax
from jax.experimental import pallas as pl
from jax.experimental.pallas import tpu as pltpu
from jax.sharding import PartitionSpec as P

MESH = pl.DeviceIdType.MESH
F32 = jnp.float32
BF16 = jnp.bfloat16

HEAD = 128
ROWS = 256
WIDTH = 8192
NV, NC, NZ = 8, 32, 8
LPD = 8
VOC = 594
PAD = 640
KVQ = 320
EPS = 1e-06
GRAD_WEIGHT = 16.0
SCALE = HEAD ** (-0.5)
FILL = -1e30

ORDERS = (
    (("x", 1), ("x", 3), ("y", 1), ("y", 3)),
    (("x", 3), ("x", 1), ("y", 3), ("y", 1)),
    (("y", 1), ("y", 3), ("x", 1), ("x", 3)),
    (("y", 3), ("y", 1), ("x", 3), ("x", 1)),
)


class Place:
    def __init__(self):
        self.v = lax.axis_index("vocab")
        self.c = lax.axis_index("ctx")
        self.xl = lax.div(self.v, 4)
        self.y = lax.rem(self.v, 4)
        self.z = lax.div(self.c, 4)
        self.xh = lax.rem(lax.div(self.c, 2), 2)
        self.core = lax.rem(self.c, 2)

    def y_off(self, off):
        y = self.y
        if off == 0:
            return y
        if off == 1:
            return y + 1 - 2 * lax.rem(y, 2)
        if off == 2:
            return lax.rem(y + 2, 4)
        return 3 - y

    def xl_off(self, off):
        return 1 - self.xl if off & 1 else self.xl

    def xh_off(self, off):
        return 1 - self.xh if off & 2 else self.xh

    def v_at(self, x_off=0, y_off=0):
        return self.xl_off(x_off) * 4 + self.y_off(y_off)

    def dev(self, x_off=0, y_off=0, z=None, core_off=0):
        z = self.z if z is None else z
        core = 1 - self.core if core_off else self.core
        return (self.v_at(x_off, y_off), z * 4 + self.xh_off(x_off) * 2 + core)

    def z_plus(self, d):
        return lax.rem(self.z + d + NZ, NZ)


def greet(devices):
    barrier = pltpu.get_barrier_semaphore()
    for device in devices:
        pl.semaphore_signal(barrier, inc=1, device_id=device, device_id_type=MESH)
    return functools.partial(pl.semaphore_wait, barrier, len(devices))


def remote(src, dst, send, recv, device):
    copy = pltpu.make_async_remote_copy(
        src_ref=src, dst_ref=dst, send_sem=send, recv_sem=recv, device_id=device, device_id_type=MESH
    )
    copy.start()
    return copy


def offsets(order, done):
    held = [(0, 0)]
    for axis, mask in order[:done]:
        held = held + [(ox ^ mask, oy) if axis == "x" else (ox, oy ^ mask) for ox, oy in held]
    return held


def partner(me, axis, mask):
    return me.dev(x_off=mask) if axis == "x" else me.dev(y_off=mask)


def gather_kernel(
    hidden, queries, keys, values, lrows, rows, kvq, z_s, z_r, a_s, a_r, f_s, f_r, k_s, k_r, kf_s, kf_r
):
    me = Place()
    mate = me.dev(core_off=1)
    greeted = greet(
        [me.dev(z=me.z_plus(d)) for d in range(1, NZ)]
        + [me.dev(x_off=1), me.dev(x_off=2), me.dev(x_off=3), me.dev(y_off=1), me.dev(y_off=3), mate]
    )
    own = lrows[me.c]
    pick = (own == lax.broadcasted_iota(jnp.int32, (LPD, hidden.shape[0]), 1)).astype(F32).astype(BF16)
    mine_cols = pl.ds(pl.multiple_of(me.v * 1024, 1024), 1024)
    rows[me.z, me.xh, me.core, :, mine_cols] = jnp.dot(
        pick, hidden[...], preferred_element_type=F32
    ).astype(BF16)
    picked_q = jnp.dot(pick, queries[...], preferred_element_type=F32).astype(BF16)
    kvq[me.z, me.xh, me.core, 0:128, :] = keys[...]
    kvq[me.z, me.xh, me.core, 128:256, :] = values[...]
    for head in range(8):
        kvq[me.z, me.xh, me.core, 256 + 8 * head : 264 + 8 * head, :] = picked_q[:, 128 * head : 128 * head + 128]
    greeted()
    started = []

    def go(*args):
        copy = remote(*args)
        started.append(copy)
        return copy

    def block(k, off):
        cols = pl.ds(pl.multiple_of(me.v_at(*off) * 1024, 1024), 1024)
        return rows.at[pl.ds(2 * k, 2), me.xh_off(off[0]), me.core, :, cols]

    own_block = rows.at[me.z, me.xh, me.core, :, mine_cols]
    z_copies = [
        go(own_block, own_block, z_s.at[d], z_r.at[d], me.dev(z=me.z_plus(d))) for d in range(1, NZ)
    ]
    own_kvq = kvq.at[me.z, me.xh, me.core]
    k_x = go(own_kvq, own_kvq, k_s.at[0], k_r.at[0], me.dev(x_off=2))
    for copy in z_copies:
        copy.wait_recv()

    a_copies = {}

    def a_step(step):
        for k, order in enumerate(ORDERS):
            axis, mask = order[step]
            for j, off in enumerate(offsets(order, step)):
                slot = (1 << step) - 1 + j
                here = block(k, off)
                a_copies[k, step, j] = go(
                    here, here, a_s.at[k, slot], a_r.at[k, slot], partner(me, axis, mask)
                )

    def forward(k, j, off):
        here = block(k, off)
        f_copies.append(go(here, here, f_s.at[k, j], f_r.at[k, j], mate))

    def a_wait(step):
        count = 1 << step
        for j in range(count):
            for k, order in enumerate(ORDERS):
                a_copies[k, step, j].wait_recv()
                forward(k, count + j, offsets(order, step + 1)[count + j])

    f_copies, kf_copies, ring = [], [], {}

    def ring_step(step):
        lo, hi = (0, KVQ) if step < 4 else (0, 160)
        lo2, hi2 = (0, KVQ) if step < 4 else (160, KVQ)
        up, down = me.z_plus(-(step - 1)), me.z_plus(step - 1)
        right = kvq.at[up, :, me.core, lo:hi]
        left = kvq.at[down, :, me.core, lo2:hi2]
        ring[step] = (
            go(right, right, k_s.at[2 * step - 1], k_r.at[2 * step - 1], me.dev(z=me.z_plus(1))),
            go(left, left, k_s.at[2 * step], k_r.at[2 * step], me.dev(z=me.z_plus(-1))),
        )

    def ring_forward(slot, z):
        here = kvq.at[z, :, me.core]
        kf_copies.append(go(here, here, kf_s.at[slot], kf_r.at[slot], mate))

    def ring_wait(step):
        ring[step][0].wait_recv()
        if step < 4:
            ring_forward(2 * step - 1, me.z_plus(-step))
        ring[step][1].wait_recv()
        ring_forward(2 * step if step < 4 else 7, me.z_plus(step))

    a_step(0)
    for k in range(4):
        forward(k, 0, (0, 0))
    k_x.wait_recv()
    ring_step(1)
    ring_forward(0, me.z)
    a_wait(0)
    a_step(1)
    a_wait(1)
    a_step(2)
    ring_wait(1)
    ring_step(2)
    a_wait(2)
    a_step(3)
    ring_wait(2)
    ring_step(3)
    a_wait(3)
    ring_wait(3)
    ring_step(4)
    ring_wait(4)
    for copy in f_copies + kf_copies:
        copy.wait_recv()
    for copy in started:
        copy.wait_send()


def gather(hidden, queries, keys, values, lrows):
    vmem = pl.BlockSpec(memory_space=pltpu.VMEM)
    dma = pltpu.SemaphoreType.DMA
    return pl.pallas_call(
        gather_kernel,
        out_shape=(
            jax.ShapeDtypeStruct((NZ, 2, 2, LPD, WIDTH), BF16),
            jax.ShapeDtypeStruct((NZ, 2, 2, KVQ, HEAD), BF16),
        ),
        in_specs=[vmem] * 5,
        out_specs=(vmem, vmem),
        scratch_shapes=[
            dma((NZ,)), dma((NZ,)), dma((4, 15)), dma((4, 15)), dma((4, 16)), dma((4, 16)),
            dma((9,)), dma((9,)), dma((8,)), dma((8,)),
        ],
        compiler_params=pltpu.CompilerParams(collective_id=0, has_side_effects=True),
        name="gather",
    )(hidden, queries, keys, values, lrows)


def column(row_vector, width=128):
    return jnp.transpose(jnp.broadcast_to(row_vector, (width, row_vector.shape[1])))


def merge(parts):
    top = jnp.max(parts[:, 0:2], axis=0)
    weight = jnp.exp(parts[:, 0:2] - top[None])
    total = jnp.sum(parts[:, 2:4] * weight, axis=0)
    first = jnp.sum(parts[:, 4:6] * weight, axis=0)
    hit = jnp.sum(parts[:, 6:8], axis=0)
    return jnp.concatenate([top, total, first, hit], axis=0)


def wide(two):
    return jnp.concatenate([two[0:1], two[1:2]], axis=1)


def loss_kernel(
    rows, gain, targets, weight_hbm, loss, resid_t, resid,
    weight, y, logits, grad_t, rms_col, inner_col, st1, st2, cs, cr, acc, sb1, sb2, sb3, sb4, rb1, rb2, rb3, rb4,
    zs, zr, w_sem, s1_s, s1_r, s2_s, s2_r, c_s, c_r, x_s, x_r, z_s, z_r, v_s, v_r,
):
    me = Place()
    mate = me.dev(core_off=1)
    group1 = [(d, o) for d in range(NZ) for o in range(2) if (d, o) != (0, 0)]
    group2 = [(ox, oy) for ox in range(4) for oy in range(4) if (ox, oy) != (0, 0)]
    greeted = greet(
        [me.dev(z=me.z_plus(d), core_off=o) for d, o in group1] + [me.dev(ox, oy) for ox, oy in group2]
    )
    loads = []
    for j in range(8):
        part = (slice(None), slice(1024 * j, 1024 * j + 1024))
        load = pltpu.make_async_copy(weight_hbm.at[part], weight.at[part], w_sem.at[j])
        load.start()
        loads.append(load)

    def prepare(j, square):
        cols = pl.ds(pl.multiple_of(j * 1024, 1024), 1024)
        x = rows[:, :, :, :, cols].astype(F32).reshape(ROWS, 1024)
        y[:, cols] = (x * gain[:, cols]).astype(BF16)
        sq = x * x
        for t in range(8):
            square = square + sq[:, 128 * t : 128 * t + 128]
        return square

    square = lax.fori_loop(0, 8, prepare, jnp.zeros((ROWS, 128), F32))
    inv_col = lax.rsqrt(jnp.sum(square, axis=1, keepdims=True) * (1.0 / WIDTH) + EPS)
    rms_col[...] = jnp.broadcast_to(inv_col, (ROWS, 128))
    inv_row = jnp.transpose(rms_col[...])[0:1, :]

    logits[PAD - 48 : PAD, :] = jnp.zeros((48, ROWS), F32)
    for j in range(8):
        loads[j].wait()
        term = lax.dot_general(
            weight[:, 1024 * j : 1024 * j + 1024], y[:, 1024 * j : 1024 * j + 1024],
            (((1,), (1,)), ((), ())), preferred_element_type=F32,
        )
        logits[0:VOC, :] = term if j == 0 else logits[0:VOC, :] + term

    ids = lax.broadcasted_iota(jnp.int32, (PAD, ROWS), 0)
    real = ids < VOC
    first_id = (me.v * NC + me.c) * VOC
    is_target = ((ids + first_id) == targets[...]) & real
    value = jnp.where(real, logits[...] * inv_row, FILL)
    logits[...] = value
    top = jnp.max(value, axis=0, keepdims=True)
    raw = jnp.exp(value - top)
    stats = (
        top,
        jnp.sum(raw, axis=0, keepdims=True),
        jnp.sum(raw * value, axis=0, keepdims=True),
        jnp.sum(jnp.where(is_target, value, 0.0), axis=0, keepdims=True),
    )
    packed = jnp.concatenate([part[:, h : h + 128] for part in stats for h in (0, 128)], axis=0)
    greeted()
    started = []

    def go(*args):
        copy = remote(*args)
        started.append(copy)
        return copy

    slot1 = me.z * 2 + me.core
    st1[slot1] = packed
    waits = []
    for i, (d, o) in enumerate(group1):
        waits.append(
            go(st1.at[slot1], st1.at[slot1], s1_s.at[i], s1_r.at[2 * d + o], me.dev(z=me.z_plus(d), core_off=o))
        )
    for copy in waits:
        copy.wait_recv()
    slot2 = (me.xh * 2 + me.xl) * 4 + me.y
    st2[slot2] = merge(st1[...])
    waits = []
    for i, (ox, oy) in enumerate(group2):
        waits.append(go(st2.at[slot2], st2.at[slot2], s2_s.at[i], s2_r.at[4 * ox + oy], me.dev(ox, oy)))
    for copy in waits:
        copy.wait_recv()
    final = merge(st2[...])
    log_total = wide(final[0:2] + jnp.log(final[2:4]))
    hit = wide(final[6:8])
    loss[...] = jnp.broadcast_to(jnp.mean(log_total - hit, axis=1, keepdims=True), (8, 128))
    inner = (wide(final[4:6] / final[2:4]) - hit) * (GRAD_WEIGHT / WIDTH)
    inner_col[...] = column(inner)
    grad = GRAD_WEIGHT * (jnp.exp(logits[...] - log_total) - is_target.astype(F32))
    grad_t[...] = jnp.transpose(grad).astype(BF16)

    def chunk(z, xh, core):
        cols = pl.ds(pl.multiple_of((z * 4 + xh * 2 + core) * 256, 256), 256)
        return jnp.dot(grad_t[:, 0:VOC], weight[:, cols], preferred_element_type=F32).reshape(NV, 32, 256)

    c_copies = []
    for k in range(4):

        def other(i, _):
            z, xh = 2 * k + lax.div(i, 2), lax.rem(i, 2)
            cs[z, xh] = chunk(z, xh, 1 - me.core).astype(BF16)
            return 0

        lax.fori_loop(0, 4, other, 0)
        part = pl.ds(2 * k, 2)
        c_copies.append(go(cs.at[part], cr.at[part], c_s.at[k], c_r.at[k], mate))

    def own(i, _):
        z, xh = lax.div(i, 2), lax.rem(i, 2)
        acc[z, xh] = chunk(z, xh, me.core)
        return 0

    lax.fori_loop(0, 16, own, 0)

    sends, recvs = (sb1, sb2, sb3, sb4), (rb1, rb2, rb3, rb4)
    moving = {}

    def at(z, off):
        return (z, me.xh_off(off[0]), me.v_at(*off))

    for step in range(4):
        for k in range(4):
            order = ORDERS[k][::-1]
            back = ORDERS[k]
            axis, mask = order[step]
            keep = offsets(back, 3 - step)
            if step == 0:
                c_copies[k].wait_recv()
            else:
                moving[k, step - 1].wait_recv()
            before = offsets(back, 4 - step)
            for z2 in range(2):
                z = 2 * k + z2
                for off in before:
                    here = at(z, off)
                    if step == 0:
                        extra = cr[here].astype(F32)
                    else:
                        extra = recvs[step - 1][k, z2, before.index(off)].astype(F32)
                    summed = acc[here] + extra
                    away = (off[0] ^ mask, off[1]) if axis == "x" else (off[0], off[1] ^ mask)
                    if away in keep:
                        sends[step][k, z2, keep.index(away)] = summed.astype(BF16)
                    else:
                        acc[here] = summed
            moving[k, step] = go(
                sends[step].at[k], recvs[step].at[k], x_s.at[k, step], x_r.at[k, step], partner(me, axis, mask)
            )
    for k in range(4):
        moving[k, 3].wait_recv()
        for z2 in range(2):
            z = 2 * k + z2
            here = at(z, (0, 0))
            summed = acc[here] + rb4[k, z2, 0].astype(F32)
            acc[here] = summed
            zs[z] = summed.astype(BF16)
    z_copies = []
    for d in range(1, NZ):
        z = me.z_plus(d)
        z_copies.append(go(zs.at[z], zr.at[me.z], z_s.at[d], z_r.at[d], me.dev(z=z)))
    zr[me.z] = zs[me.z]
    for copy in z_copies:
        copy.wait_recv()
    normed_grad = jnp.sum(zr[...].astype(F32), axis=0)
    cols = pl.ds(pl.multiple_of(me.c * 256, 256), 256)
    lines = pl.ds(pl.multiple_of(me.v * 32, 32), 32)
    inv = rms_col[lines, 0:1]
    picked = rows[me.v, :, :, :, cols].astype(F32).reshape(32, 256)
    out = inv * (normed_grad * gain[:, cols] - picked * (inv * inner_col[lines, 0:1]))
    resid[me.v] = out.astype(BF16)
    v_copies = []
    for i, (ox, oy) in enumerate([(o, q) for o in range(2) for q in range(4) if (o, q) != (0, 0)]):
        v_copies.append(go(resid.at[me.v], resid.at[me.v], v_s.at[i], v_r.at[i], me.dev(ox, oy)))
    for copy in v_copies:
        copy.wait_recv()
    resid_t[...] = jnp.transpose(resid[...].astype(F32).reshape(ROWS, 256)).astype(BF16)
    for copy in started:
        copy.wait_send()


def loss_part(rows, gain, targets, head_weight):
    vmem = pl.BlockSpec(memory_space=pltpu.VMEM)
    dma = pltpu.SemaphoreType.DMA
    scratch = pltpu.VMEM
    halves = [8, 4, 2, 1]
    return pl.pallas_call(
        loss_kernel,
        out_shape=(
            jax.ShapeDtypeStruct((8, 128), F32),
            jax.ShapeDtypeStruct((256, ROWS), BF16),
            jax.ShapeDtypeStruct((NV, 32, 256), BF16),
        ),
        in_specs=[vmem, vmem, vmem, pl.BlockSpec(memory_space=pl.ANY)],
        out_specs=(vmem, vmem, vmem),
        scratch_shapes=[
            scratch((VOC, WIDTH), BF16),
            scratch((ROWS, WIDTH), BF16),
            scratch((PAD, ROWS), F32),
            scratch((ROWS, PAD), BF16),
            scratch((ROWS, 128), F32),
            scratch((ROWS, 128), F32),
            scratch((16, 8, 128), F32),
            scratch((16, 8, 128), F32),
            scratch((NZ, 2, NV, 32, 256), BF16),
            scratch((NZ, 2, NV, 32, 256), BF16),
            scratch((NZ, 2, NV, 32, 256), F32),
            *[scratch((4, 2, n, 32, 256), BF16) for n in halves],
            *[scratch((4, 2, n, 32, 256), BF16) for n in halves],
            scratch((NZ, 32, 256), BF16),
            scratch((NZ, 32, 256), BF16),
            dma((8,)),
            dma((16,)), dma((16,)), dma((16,)), dma((16,)), dma((4,)), dma((4,)),
            dma((4, 4)), dma((4, 4)), dma((NZ,)), dma((NZ,)), dma((7,)), dma((7,)),
        ],
        compiler_params=pltpu.CompilerParams(
            collective_id=1, has_side_effects=True, vmem_limit_bytes=60 * 1024 * 1024
        ),
        name="loss_part",
    )(rows, gain, targets, head_weight)


def attention_kernel(
    resid, out_weight, kvq, key_pos, query_pos, key_col, query_col, dq, dk, dv,
    k_all, v_all, probs, part, cr, acc, rs, rr, grads, extras, st, s2, q_all,
    c_s, c_r, r_s, r_r, g_s, g_r, e_s, e_r, fg_s, fg_r, fe_s, fe_r,
):
    me = Place()
    mate = me.dev(core_off=1)
    peers = [(d, o) for d in range(NZ) for o in (0, 2) if (d, o) != (0, 0)]
    greeted = greet([me.dev(z=me.z_plus(d), x_off=o) for d, o in peers] + [mate])
    started = []

    def go(*args):
        copy = remote(*args)
        started.append(copy)
        return copy

    wide_part = lax.dot_general(
        resid[...].reshape(ROWS, 256), out_weight[...], (((1,), (1,)), ((), ())), preferred_element_type=F32
    )
    for h in range(8):
        part[:, :, :, 8 * h : 8 * h + 8, :] = wide_part[:, 128 * h : 128 * h + 128].reshape(NZ, 2, 2, LPD, HEAD)
    cs = acc
    cs[...] = part[:, :, 1 - me.core].astype(BF16)
    greeted()
    c_copy = go(cs, cr, c_s, c_r, mate)

    k_all[...] = kvq[:, :, :, 0:128, :].reshape(NC * 128, HEAD)
    v_all[...] = kvq[:, :, :, 128:256, :].reshape(NC * 128, HEAD)
    q_all[...] = kvq[:, :, :, 256:320, :].reshape(NC * 64, HEAD)
    q_own = kvq[me.z, me.xh, me.core, 256:320, :]
    c_copy.wait_recv()
    rs[...] = (part[:, :, me.core] + cr[...].astype(F32)).astype(BF16)
    r_copies = []
    for i, (d, o) in enumerate(peers):
        z, xh = me.z_plus(d), me.xh_off(o)
        r_copies.append(
            go(rs.at[z, xh], rr.at[me.z, me.xh], r_s.at[i], r_r.at[i], me.dev(z=z, x_off=o))
        )
    rr[me.z, me.xh] = rs[me.z, me.xh]
    scores = lax.dot_general(q_own, k_all[...], (((1,), (1,)), ((), ())), preferred_element_type=F32)
    seen = key_pos[...] <= query_col[...]
    masked = jnp.where(seen, scores * SCALE, FILL)
    top = jnp.max(masked, axis=1, keepdims=True)
    raw = jnp.where(seen, jnp.exp(masked - top), 0.0)
    total = jnp.sum(raw, axis=1, keepdims=True)
    probs[...] = raw / total
    log_total = top + jnp.log(total)
    high = probs[...].astype(BF16)
    low = (probs[...] - high.astype(F32)).astype(BF16)
    out = jnp.dot(high, v_all[...], preferred_element_type=F32) + jnp.dot(
        low, v_all[...], preferred_element_type=F32
    )
    k_own = kvq[me.z, me.xh, me.core, 0:128, :]
    v_own = kvq[me.z, me.xh, me.core, 128:256, :]
    s2[...] = lax.dot_general(k_own, q_all[...], (((1,), (1,)), ((), ())), preferred_element_type=F32)
    for copy in r_copies:
        copy.wait_recv()
    grad_own = jnp.sum(rr[...].astype(F32), axis=(0, 1)).astype(BF16)
    grads[me.z, me.xh, me.core] = grad_own
    delta = jnp.sum(grad_own.astype(F32) * out, axis=1, keepdims=True)
    lane = lax.broadcasted_iota(jnp.int32, (64, 128), 1)
    both = jnp.where(lane == 0, delta, jnp.where(lane == 1, log_total, 0.0))
    st[...] = jnp.zeros((128, 128), F32)
    st[0:64, :] = both
    extras[me.z, me.xh, me.core] = jnp.transpose(st[...])[0:8, :]
    own_g, own_e = grads.at[me.z, me.xh, me.core], extras.at[me.z, me.xh, me.core]
    g_copies = []
    for i, (d, o) in enumerate(peers):
        device = me.dev(z=me.z_plus(d), x_off=o)
        g_copies.append(
            (
                go(own_g, own_g, g_s.at[i], g_r.at[i], device),
                go(own_e, own_e, e_s.at[i], e_r.at[i], device),
                d,
                o,
            )
        )
    forwards = [
        go(own_g, own_g, fg_s.at[15], fg_r.at[15], mate),
        go(own_e, own_e, fe_s.at[15], fe_r.at[15], mate),
    ]
    prob_grad = lax.dot_general(grad_own, v_all[...], (((1,), (1,)), ((), ())), preferred_element_type=F32)
    score_grad = (probs[...] * (prob_grad - delta)).astype(BF16)
    query_grad = (jnp.dot(score_grad, k_all[...], preferred_element_type=F32) * SCALE).astype(F32)
    for h in range(8):
        dq[:, 128 * h : 128 * h + 128] = query_grad[8 * h : 8 * h + 8, :].astype(BF16)
    for i, (g_copy, e_copy, d, o) in enumerate(g_copies):
        z, xh = me.z_plus(-d), me.xh_off(o)
        g_copy.wait_recv()
        e_copy.wait_recv()
        here_g, here_e = grads.at[z, xh, me.core], extras.at[z, xh, me.core]
        forwards.append(go(here_g, here_g, fg_s.at[i], fg_r.at[i], mate))
        forwards.append(go(here_e, here_e, fe_s.at[i], fe_r.at[i], mate))
    for copy in forwards:
        copy.wait_recv()
    grads_all = grads[...].reshape(NC * 64, HEAD)
    e_all = extras[...].reshape(NC, 8, 128)
    delta_all = jnp.concatenate([e_all[i, 0:1, 0:64] for i in range(NC)], axis=1)
    log_all = jnp.concatenate([e_all[i, 1:2, 0:64] for i in range(NC)], axis=1)
    seen2 = key_col[...] <= query_pos[...]
    probs2 = jnp.where(seen2, jnp.exp(s2[...] * SCALE - log_all), 0.0)
    dv[...] = jnp.dot(probs2.astype(BF16), grads_all, preferred_element_type=F32).astype(BF16)
    prob_grad2 = lax.dot_general(v_own, grads_all, (((1,), (1,)), ((), ())), preferred_element_type=F32)
    score_grad2 = (probs2 * (prob_grad2 - delta_all)).astype(BF16)
    dk[...] = (jnp.dot(score_grad2, q_all[...], preferred_element_type=F32) * SCALE).astype(BF16)
    for copy in started:
        copy.wait_send()


def attention_part(resid, out_weight, kvq, key_pos, query_pos, key_col, query_col):
    vmem = pl.BlockSpec(memory_space=pltpu.VMEM)
    dma = pltpu.SemaphoreType.DMA
    scratch = pltpu.VMEM
    return pl.pallas_call(
        attention_kernel,
        out_shape=(
            jax.ShapeDtypeStruct((LPD, 1024), BF16),
            jax.ShapeDtypeStruct((128, HEAD), BF16),
            jax.ShapeDtypeStruct((128, HEAD), BF16),
        ),
        in_specs=[vmem] * 7,
        out_specs=(vmem, vmem, vmem),
        scratch_shapes=[
            scratch((NC * 128, HEAD), BF16),
            scratch((NC * 128, HEAD), BF16),
            scratch((64, NC * 128), F32),
            scratch((NZ, 2, 2, 64, HEAD), F32),
            scratch((NZ, 2, 64, HEAD), BF16),
            scratch((NZ, 2, 64, HEAD), BF16),
            scratch((NZ, 2, 64, HEAD), BF16),
            scratch((NZ, 2, 64, HEAD), BF16),
            scratch((NZ, 2, 2, 64, HEAD), BF16),
            scratch((NZ, 2, 2, 8, 128), F32),
            scratch((128, 128), F32),
            scratch((128, NC * 64), F32),
            scratch((NC * 64, HEAD), BF16),
            dma, dma, dma((15,)), dma((15,)), dma((15,)), dma((15,)), dma((15,)), dma((15,)),
            dma((16,)), dma((16,)), dma((16,)), dma((16,)),
        ],
        compiler_params=pltpu.CompilerParams(
            collective_id=2, has_side_effects=True, vmem_limit_bytes=60 * 1024 * 1024
        ),
        name="attention_part",
    )(resid, out_weight, kvq, key_pos, query_pos, key_col, query_col)


def per_device(
    hidden,
    norm_gain,
    head_weight,
    targets,
    loss_rows,
    stretch_of_slot,
    queries,
    key_states,
    attention_values,
    output_weight,
):
    c = lax.axis_index("ctx")
    spans = stretch_of_slot.reshape(NC, 2)
    local = loss_rows.reshape(NC, LPD)
    place = jnp.where(local < 64, spans[:, 0:1], spans[:, 1:2]) * 64 + lax.rem(local, 64)
    query_pos = jnp.broadcast_to(place[:, None, :], (NC, 8, LPD)).reshape(1, NC * 64)
    query_col = lax.dynamic_slice_in_dim(query_pos, c * 64, 64, 1).reshape(64, 1)
    key_pos = (stretch_of_slot[:, None] * 64 + lax.broadcasted_iota(jnp.int32, (64, 64), 1)).reshape(1, 4096)
    key_col = lax.dynamic_slice_in_dim(key_pos, c * 128, 128, 1).reshape(128, 1)
    rows, kvq = gather(hidden, queries, key_states, attention_values, loss_rows.reshape(NC, LPD, 1))
    loss, resid_t, resid = loss_part(
        rows, norm_gain.reshape(1, WIDTH), targets.reshape(1, ROWS), head_weight
    )
    dq, dk, dv = attention_part(resid, output_weight, kvq, key_pos, query_pos, key_col, query_col)
    return (loss[0, 0], dq, dk, dv, resid_t)


def solution(mesh):
    placed = (
        P("ctx", "vocab"),
        P(),
        P(("vocab", "ctx"), None),
        P(),
        P(),
        P(),
        P("ctx", "vocab"),
        P("ctx", "vocab"),
        P("ctx", "vocab"),
        P("vocab", "ctx"),
    )
    return jax.shard_map(
        per_device,
        mesh=mesh,
        in_specs=placed,
        out_specs=(P(), P("ctx", "vocab"), P("ctx", "vocab"), P("ctx", "vocab"), P("ctx", None)),
        check_vma=False,
    )
```

```python
import functools

import jax
import jax.numpy as jnp
from jax import lax
from jax.experimental import pallas as pl
from jax.experimental.pallas import tpu as pltpu
from jax.sharding import PartitionSpec as P

MESH = pl.DeviceIdType.MESH
F32 = jnp.float32
BF16 = jnp.bfloat16

HEAD = 128
ROWS = 256
WIDTH = 8192
NV, NC, NZ = 8, 32, 8
LPD = 8
VOC = 594
PAD = 640
KVQ = 320
EPS = 1e-06
GRAD_WEIGHT = 16.0
SCALE = HEAD ** (-0.5)
FILL = -1e30

ORDERS = (
    (("x", 1), ("x", 3), ("y", 1), ("y", 3)),
    (("x", 3), ("x", 1), ("y", 3), ("y", 1)),
    (("y", 1), ("y", 3), ("x", 1), ("x", 3)),
    (("y", 3), ("y", 1), ("x", 3), ("x", 1)),
)


class Place:
    def __init__(self):
        self.v = lax.axis_index("vocab")
        self.c = lax.axis_index("ctx")
        self.xl = lax.div(self.v, 4)
        self.y = lax.rem(self.v, 4)
        self.z = lax.div(self.c, 4)
        self.xh = lax.rem(lax.div(self.c, 2), 2)
        self.core = lax.rem(self.c, 2)

    def y_off(self, off):
        y = self.y
        if off == 0:
            return y
        if off == 1:
            return y + 1 - 2 * lax.rem(y, 2)
        if off == 2:
            return lax.rem(y + 2, 4)
        return 3 - y

    def xl_off(self, off):
        return 1 - self.xl if off & 1 else self.xl

    def xh_off(self, off):
        return 1 - self.xh if off & 2 else self.xh

    def v_at(self, x_off=0, y_off=0):
        return self.xl_off(x_off) * 4 + self.y_off(y_off)

    def dev(self, x_off=0, y_off=0, z=None, core_off=0):
        z = self.z if z is None else z
        core = 1 - self.core if core_off else self.core
        return (self.v_at(x_off, y_off), z * 4 + self.xh_off(x_off) * 2 + core)

    def z_plus(self, d):
        return lax.rem(self.z + d + NZ, NZ)


def greet(devices):
    barrier = pltpu.get_barrier_semaphore()
    for device in devices:
        pl.semaphore_signal(barrier, inc=1, device_id=device, device_id_type=MESH)
    return functools.partial(pl.semaphore_wait, barrier, len(devices))


def remote(src, dst, send, recv, device):
    copy = pltpu.make_async_remote_copy(
        src_ref=src, dst_ref=dst, send_sem=send, recv_sem=recv, device_id=device, device_id_type=MESH
    )
    copy.start()
    return copy


def offsets(order, done):
    held = [(0, 0)]
    for axis, mask in order[:done]:
        held = held + [(ox ^ mask, oy) if axis == "x" else (ox, oy ^ mask) for ox, oy in held]
    return held


def partner(me, axis, mask):
    return me.dev(x_off=mask) if axis == "x" else me.dev(y_off=mask)


def column(row_vector, width=128):
    return jnp.transpose(jnp.broadcast_to(row_vector, (width, row_vector.shape[1])))


def merge(parts):
    top = jnp.max(parts[:, 0:2], axis=0)
    weight = jnp.exp(parts[:, 0:2] - top[None])
    total = jnp.sum(parts[:, 2:4] * weight, axis=0)
    first = jnp.sum(parts[:, 4:6] * weight, axis=0)
    hit = jnp.sum(parts[:, 6:8], axis=0)
    return jnp.concatenate([top, total, first, hit], axis=0)


def wide(two):
    return jnp.concatenate([two[0:1], two[1:2]], axis=1)


def step_kernel(
    hidden, queries, keys, values, lrows, targets, gain, key_pos, query_pos, out_weight, weight_hbm,
    loss, resid_t, dq, dk, dv,
    weight, rows, y, kvq, logits, grad_t, rms_col, inner_col, st1, st2, cs, cr, acc,
    sb1, sb2, sb3, sb4, rb1, rb2, rb3, rb4, zs, zr, resid,
    k_all, v_all, q_all, probs, part, pc, pr, rs, rr, grads, extras, square_tile, s2,
    w_sem, z_s, z_r, a_s, a_r, f_s, f_r, k_s, k_r, kf_s, kf_r, s1_s, s1_r, s2_s, s2_r,
    c_s, c_r, x_s, x_r, t_s, t_r, v_s, v_r, pc_s, pc_r, r_s, r_r, g_s, g_r, e_s, e_r, fg_s, fg_r, fe_s, fe_r,
):
    me = Place()
    mate = me.dev(core_off=1)
    group1 = [(d, o) for d in range(NZ) for o in range(2) if (d, o) != (0, 0)]
    group2 = [(ox, oy) for ox in range(4) for oy in range(4) if (ox, oy) != (0, 0)]
    peers = [(d, o) for d in range(NZ) for o in (0, 2) if (d, o) != (0, 0)]
    greeted = greet(
        [me.dev(z=me.z_plus(d), core_off=o) for d, o in group1]
        + [me.dev(ox, oy) for ox, oy in group2]
        + [me.dev(z=me.z_plus(d), x_off=2) for d in range(1, NZ)]
    )
    loads = []
    for j in range(8):
        section = (slice(None), slice(1024 * j, 1024 * j + 1024))
        load = pltpu.make_async_copy(weight_hbm.at[section], weight.at[section], w_sem.at[j])
        load.start()
        loads.append(load)
    started = []

    def go(*args):
        copy = remote(*args)
        started.append(copy)
        return copy

    lane = lax.broadcasted_iota(jnp.int32, (LPD, ROWS), 1)
    line = lax.broadcasted_iota(jnp.int32, (LPD, ROWS), 0)
    own = jnp.sum(jnp.where(lane == me.c * LPD + line, lrows[...], 0.0), axis=1, keepdims=True)
    rows_at = lax.broadcasted_iota(jnp.int32, (LPD, 128), 1).astype(F32)
    pick = (own == rows_at).astype(F32).astype(BF16)
    mine_cols = pl.ds(pl.multiple_of(me.v * 1024, 1024), 1024)
    rows[me.z, me.xh, me.core, :, mine_cols] = jnp.dot(
        pick, hidden[...], preferred_element_type=F32
    ).astype(BF16)
    picked_q = jnp.dot(pick, queries[...], preferred_element_type=F32).astype(BF16)
    kvq[me.z, me.xh, me.core, 0:128, :] = keys[...]
    kvq[me.z, me.xh, me.core, 128:256, :] = values[...]
    for head in range(8):
        kvq[me.z, me.xh, me.core, 256 + 8 * head : 264 + 8 * head, :] = picked_q[:, 128 * head : 128 * head + 128]
    greeted()

    def block(k, off):
        cols = pl.ds(pl.multiple_of(me.v_at(*off) * 1024, 1024), 1024)
        return rows.at[pl.ds(2 * k, 2), me.xh_off(off[0]), me.core, :, cols]

    own_block = rows.at[me.z, me.xh, me.core, :, mine_cols]
    z_copies = [
        go(own_block, own_block, z_s.at[d], z_r.at[d], me.dev(z=me.z_plus(d))) for d in range(1, NZ)
    ]
    own_kvq = kvq.at[me.z, me.xh, me.core]
    k_x = go(own_kvq, own_kvq, k_s.at[0], k_r.at[0], me.dev(x_off=2))
    for copy in z_copies:
        copy.wait_recv()

    a_copies, f_copies, kf_copies, ring = {}, [], [], {}

    def spread(k, index, off, first):
        here = block(k, off)
        for step in range(first, 4):
            slot = (1 << step) - 1 + index
            a_copies[k, step, index] = go(
                here, here, a_s.at[k, slot], a_r.at[k, slot], partner(me, *ORDERS[k][step])
            )
        f_copies.append(go(here, here, f_s.at[k, index], f_r.at[k, index], mate))

    def arrive(step, js):
        for j in js:
            for k, order in enumerate(ORDERS):
                a_copies[k, step, j].wait_recv()
                index = (1 << step) + j
                spread(k, index, offsets(order, step + 1)[index], step + 1)

    def ring_step(step):
        lo, hi = (0, KVQ) if step < 4 else (0, 160)
        lo2, hi2 = (0, KVQ) if step < 4 else (160, KVQ)
        up, down = me.z_plus(-(step - 1)), me.z_plus(step - 1)
        right = kvq.at[up, :, me.core, lo:hi]
        left = kvq.at[down, :, me.core, lo2:hi2]
        ring[step] = (
            go(right, right, k_s.at[2 * step - 1], k_r.at[2 * step - 1], me.dev(z=me.z_plus(1))),
            go(left, left, k_s.at[2 * step], k_r.at[2 * step], me.dev(z=me.z_plus(-1))),
        )

    def ring_forward(slot, z):
        here = kvq.at[z, :, me.core]
        kf_copies.append(go(here, here, kf_s.at[slot], kf_r.at[slot], mate))

    def ring_wait(step):
        ring[step][0].wait_recv()
        if step < 4:
            ring_forward(2 * step - 1, me.z_plus(-step))
        ring[step][1].wait_recv()
        ring_forward(2 * step if step < 4 else 7, me.z_plus(step))

    for k in range(4):
        spread(k, 0, (0, 0), 0)
    arrive(0, range(1))
    k_x.wait_recv()
    ring_step(1)
    ring_forward(0, me.z)
    arrive(1, range(2))
    arrive(2, range(4))
    ring_wait(1)
    ring_step(2)
    arrive(3, range(4))
    ring_wait(2)
    ring_step(3)
    arrive(3, range(4, 8))
    for copy in f_copies:
        copy.wait_recv()

    def prepare(j, square):
        cols = pl.ds(pl.multiple_of(j * 1024, 1024), 1024)
        x = rows[:, :, :, :, cols].astype(F32).reshape(ROWS, 1024)
        y[:, cols] = (x * gain[:, cols]).astype(BF16)
        sq = x * x
        for t in range(8):
            square = square + sq[:, 128 * t : 128 * t + 128]
        return square

    square = lax.fori_loop(0, 8, prepare, jnp.zeros((ROWS, 128), F32))
    inv_col = lax.rsqrt(jnp.sum(square, axis=1, keepdims=True) * (1.0 / WIDTH) + EPS)
    rms_col[...] = jnp.broadcast_to(inv_col, (ROWS, 128))
    inv_row = jnp.transpose(rms_col[...])[0:1, :]

    logits[PAD - 48 : PAD, :] = jnp.zeros((48, ROWS), F32)
    for j in range(8):
        loads[j].wait()
        term = lax.dot_general(
            weight[:, 1024 * j : 1024 * j + 1024], y[:, 1024 * j : 1024 * j + 1024],
            (((1,), (1,)), ((), ())), preferred_element_type=F32,
        )
        logits[0:VOC, :] = term if j == 0 else logits[0:VOC, :] + term
        if j == 3:
            ring_wait(3)
            ring_step(4)

    ids = lax.broadcasted_iota(jnp.int32, (PAD, ROWS), 0)
    real = ids < VOC
    first_id = (me.v * NC + me.c) * VOC
    is_target = ((ids + first_id) == targets[...]) & real
    value = jnp.where(real, logits[...] * inv_row, FILL)
    logits[...] = value
    top = jnp.max(value, axis=0, keepdims=True)
    raw = jnp.exp(value - top)
    stats = (
        top,
        jnp.sum(raw, axis=0, keepdims=True),
        jnp.sum(raw * value, axis=0, keepdims=True),
        jnp.sum(jnp.where(is_target, value, 0.0), axis=0, keepdims=True),
    )
    packed = jnp.concatenate([piece[:, h : h + 128] for piece in stats for h in (0, 128)], axis=0)
    slot1 = me.z * 2 + me.core
    st1[slot1] = packed
    waits = []
    for i, (d, o) in enumerate(group1):
        waits.append(
            go(st1.at[slot1], st1.at[slot1], s1_s.at[i], s1_r.at[2 * d + o], me.dev(z=me.z_plus(d), core_off=o))
        )
    ring_wait(4)
    for copy in kf_copies:
        copy.wait_recv()

    k_all[...] = kvq[:, :, :, 0:128, :].reshape(NC * 128, HEAD)
    v_all[...] = kvq[:, :, :, 128:256, :].reshape(NC * 128, HEAD)
    q_all[...] = kvq[:, :, :, 256:320, :].reshape(NC * 64, HEAD)
    q_own = kvq[me.z, me.xh, me.core, 256:320, :]
    lane = lax.broadcasted_iota(jnp.int32, (64, NC * 64), 1)
    line = lax.broadcasted_iota(jnp.int32, (64, NC * 64), 0)
    query_col = jnp.sum(jnp.where(lane == me.c * 64 + line, query_pos[...], 0.0), axis=1, keepdims=True)
    for copy in waits:
        copy.wait_recv()
    slot2 = (me.xh * 2 + me.xl) * 4 + me.y
    st2[slot2] = merge(st1[...])
    waits = []
    for i, (ox, oy) in enumerate(group2):
        waits.append(go(st2.at[slot2], st2.at[slot2], s2_s.at[i], s2_r.at[4 * ox + oy], me.dev(ox, oy)))
    scores = lax.dot_general(q_own, k_all[...], (((1,), (1,)), ((), ())), preferred_element_type=F32)
    seen = key_pos[...] <= query_col
    masked = jnp.where(seen, scores * SCALE, FILL)
    top = jnp.max(masked, axis=1, keepdims=True)
    raw = jnp.where(seen, jnp.exp(masked - top), 0.0)
    total = jnp.sum(raw, axis=1, keepdims=True)
    probs[...] = raw / total
    row_log_total = top + jnp.log(total)

    for copy in waits:
        copy.wait_recv()
    final = merge(st2[...])
    log_total = wide(final[0:2] + jnp.log(final[2:4]))
    hit = wide(final[6:8])
    grad = GRAD_WEIGHT * (jnp.exp(logits[...] - log_total) - is_target.astype(F32))
    grad_t[...] = jnp.transpose(grad).astype(BF16)

    def chunk(z, xh, core):
        cols = pl.ds(pl.multiple_of((z * 4 + xh * 2 + core) * 256, 256), 256)
        return jnp.dot(grad_t[:, 0:VOC], weight[:, cols], preferred_element_type=F32).reshape(NV, 32, 256)

    c_copies = {}
    z_order = (0, 2, 4, 6, 1, 3, 5, 7)
    for z in z_order:

        def other(xh, _, z=z):
            cs[z, xh] = chunk(z, xh, 1 - me.core).astype(BF16)
            return 0

        lax.fori_loop(0, 2, other, 0)
        c_copies[z] = go(cs.at[z], cr.at[z], c_s.at[z], c_r.at[z], mate)

    sends, recvs = (sb1, sb2, sb3, sb4), (rb1, rb2, rb3, rb4)
    moving = {}

    def at(z, off):
        return (z, me.xh_off(off[0]), me.v_at(*off))

    def halve(z, step):
        back = ORDERS[z // 2]
        axis, mask = back[3 - step]
        keep, before = offsets(back, 3 - step), offsets(back, 4 - step)
        for off in before:
            here = at(z, off)
            if step == 0:
                extra = cr[here].astype(F32)
            else:
                extra = recvs[step - 1][z, before.index(off)].astype(F32)
            summed = acc[here] + extra
            away = (off[0] ^ mask, off[1]) if axis == "x" else (off[0], off[1] ^ mask)
            if away in keep:
                sends[step][z, keep.index(away)] = summed.astype(BF16)
            else:
                acc[here] = summed
        moving[z, step] = go(
            sends[step].at[z], recvs[step].at[z], x_s.at[z, step], x_r.at[z, step], partner(me, axis, mask)
        )

    for z in z_order:

        def mine(xh, _, z=z):
            acc[z, xh] = chunk(z, xh, me.core)
            return 0

        lax.fori_loop(0, 2, mine, 0)
        c_copies[z].wait_recv()
        halve(z, 0)
    for step in range(1, 4):
        for z in z_order:
            moving[z, step - 1].wait_recv()
            halve(z, step)

    def z_copy(z, src):
        return pltpu.make_async_remote_copy(
            src_ref=zs.at[z], dst_ref=zr.at[src], send_sem=t_s.at[z], recv_sem=t_r.at[src],
            device_id=me.dev(z=jnp.int32(z)), device_id_type=MESH,
        )

    for z in z_order:
        moving[z, 3].wait_recv()
        zs[z] = (acc[at(z, (0, 0))] + rb4[z, 0].astype(F32)).astype(BF16)

        @pl.when(me.z != z)
        def _(z=z):
            z_copy(z, me.z).start()

    loss[...] = jnp.broadcast_to(jnp.mean(log_total - hit, axis=1, keepdims=True), (8, 128))
    inner_col[...] = column((wide(final[4:6] / final[2:4]) - hit) * (GRAD_WEIGHT / WIDTH))
    k_own = kvq[me.z, me.xh, me.core, 0:128, :]
    v_own = kvq[me.z, me.xh, me.core, 128:256, :]
    s2[...] = lax.dot_general(k_own, q_all[...], (((1,), (1,)), ((), ())), preferred_element_type=F32)
    zr[me.z] = zs[me.z]
    for z in range(NZ):

        @pl.when(me.z != z)
        def _(z=z):
            z_copy(z, z).wait_recv()

    normed_grad = jnp.sum(zr[...].astype(F32), axis=0)
    cols = pl.ds(pl.multiple_of(me.c * 256, 256), 256)
    lines = pl.ds(pl.multiple_of(me.v * 32, 32), 32)
    inv = rms_col[lines, 0:1]
    picked = rows[me.v, :, :, :, cols].astype(F32).reshape(32, 256)
    out = inv * (normed_grad * gain[:, cols] - picked * (inv * inner_col[lines, 0:1]))
    resid[me.v] = out.astype(BF16)
    v_copies = []
    for i, (ox, oy) in enumerate([(o, q) for o in range(2) for q in range(4) if (o, q) != (0, 0)]):
        v_copies.append(go(resid.at[me.v], resid.at[me.v], v_s.at[i], v_r.at[i], me.dev(ox, oy)))
    high = probs[...].astype(BF16)
    low = (probs[...] - high.astype(F32)).astype(BF16)
    attn_out = jnp.dot(high, v_all[...], preferred_element_type=F32) + jnp.dot(
        low, v_all[...], preferred_element_type=F32
    )
    for copy in v_copies:
        copy.wait_recv()

    wide_part = lax.dot_general(
        resid[...].reshape(ROWS, 256), out_weight[...], (((1,), (1,)), ((), ())), preferred_element_type=F32
    )
    for h in range(8):
        part[:, :, :, 8 * h : 8 * h + 8, :] = wide_part[:, 128 * h : 128 * h + 128].reshape(NZ, 2, 2, LPD, HEAD)
    pc[...] = part[:, :, 1 - me.core].astype(BF16)
    pc_copy = go(pc, pr, pc_s, pc_r, mate)
    resid_t[...] = jnp.transpose(resid[...].astype(F32).reshape(ROWS, 256)).astype(BF16)
    pc_copy.wait_recv()
    rs[...] = (part[:, :, me.core] + pr[...].astype(F32)).astype(BF16)
    r_copies = []
    for i, (d, o) in enumerate(peers):
        z, xh = me.z_plus(d), me.xh_off(o)
        r_copies.append(go(rs.at[z, xh], rr.at[me.z, me.xh], r_s.at[i], r_r.at[i], me.dev(z=z, x_off=o)))
    rr[me.z, me.xh] = rs[me.z, me.xh]
    for copy in r_copies:
        copy.wait_recv()
    grad_own = jnp.sum(rr[...].astype(F32), axis=(0, 1)).astype(BF16)
    grads[me.z, me.xh, me.core] = grad_own
    delta = jnp.sum(grad_own.astype(F32) * attn_out, axis=1, keepdims=True)
    lane = lax.broadcasted_iota(jnp.int32, (64, 128), 1)
    square_tile[...] = jnp.zeros((128, 128), F32)
    square_tile[0:64, :] = jnp.where(lane == 0, delta, jnp.where(lane == 1, row_log_total, 0.0))
    extras[me.z, me.xh, me.core] = jnp.transpose(square_tile[...])[0:8, :]
    own_g, own_e = grads.at[me.z, me.xh, me.core], extras.at[me.z, me.xh, me.core]
    g_copies = []
    for i, (d, o) in enumerate(peers):
        device = me.dev(z=me.z_plus(d), x_off=o)
        g_copies.append(
            (
                go(own_g, own_g, g_s.at[i], g_r.at[i], device),
                go(own_e, own_e, e_s.at[i], e_r.at[i], device),
                d,
                o,
            )
        )
    forwards = [
        go(own_g, own_g, fg_s.at[15], fg_r.at[15], mate),
        go(own_e, own_e, fe_s.at[15], fe_r.at[15], mate),
    ]
    prob_grad = lax.dot_general(grad_own, v_all[...], (((1,), (1,)), ((), ())), preferred_element_type=F32)
    score_grad = (probs[...] * (prob_grad - delta)).astype(BF16)
    query_grad = jnp.dot(score_grad, k_all[...], preferred_element_type=F32) * SCALE
    for h in range(8):
        dq[:, 128 * h : 128 * h + 128] = query_grad[8 * h : 8 * h + 8, :].astype(BF16)
    for i, (g_copy, e_copy, d, o) in enumerate(g_copies):
        z, xh = me.z_plus(-d), me.xh_off(o)
        g_copy.wait_recv()
        e_copy.wait_recv()
        here_g, here_e = grads.at[z, xh, me.core], extras.at[z, xh, me.core]
        forwards.append(go(here_g, here_g, fg_s.at[i], fg_r.at[i], mate))
        forwards.append(go(here_e, here_e, fe_s.at[i], fe_r.at[i], mate))
    own_key_pos = key_pos[:, pl.ds(pl.multiple_of(me.c * 128, 128), 128)]
    lane = lax.broadcasted_iota(jnp.int32, (128, 128), 1)
    line = lax.broadcasted_iota(jnp.int32, (128, 128), 0)
    key_col = jnp.sum(jnp.where(lane == line, own_key_pos, 0.0), axis=1, keepdims=True)
    seen2 = key_col <= query_pos[...]
    for copy in forwards:
        copy.wait_recv()
    grads_all = grads[...].reshape(NC * 64, HEAD)
    e_all = extras[...].reshape(NC, 8, 128)
    delta_all = jnp.concatenate([e_all[i, 0:1, 0:64] for i in range(NC)], axis=1)
    log_all = jnp.concatenate([e_all[i, 1:2, 0:64] for i in range(NC)], axis=1)
    probs2 = jnp.where(seen2, jnp.exp(s2[...] * SCALE - log_all), 0.0)
    dv[...] = jnp.dot(probs2.astype(BF16), grads_all, preferred_element_type=F32).astype(BF16)
    prob_grad2 = lax.dot_general(v_own, grads_all, (((1,), (1,)), ((), ())), preferred_element_type=F32)
    score_grad2 = (probs2 * (prob_grad2 - delta_all)).astype(BF16)
    dk[...] = (jnp.dot(score_grad2, q_all[...], preferred_element_type=F32) * SCALE).astype(BF16)
    for copy in started:
        copy.wait_send()
    for z in range(NZ):

        @pl.when(me.z != z)
        def _(z=z):
            z_copy(z, me.z).wait_send()


def step(*operands):
    vmem = pl.BlockSpec(memory_space=pltpu.VMEM)
    dma = pltpu.SemaphoreType.DMA
    scratch = pltpu.VMEM
    halves = [8, 4, 2, 1]
    return pl.pallas_call(
        step_kernel,
        out_shape=(
            jax.ShapeDtypeStruct((8, 128), F32),
            jax.ShapeDtypeStruct((256, ROWS), BF16),
            jax.ShapeDtypeStruct((LPD, 1024), BF16),
            jax.ShapeDtypeStruct((128, HEAD), BF16),
            jax.ShapeDtypeStruct((128, HEAD), BF16),
        ),
        in_specs=[vmem] * 10 + [pl.BlockSpec(memory_space=pl.ANY)],
        out_specs=(vmem,) * 5,
        scratch_shapes=[
            scratch((VOC, WIDTH), BF16),
            scratch((NZ, 2, 2, LPD, WIDTH), BF16),
            scratch((ROWS, WIDTH), BF16),
            scratch((NZ, 2, 2, KVQ, HEAD), BF16),
            scratch((PAD, ROWS), F32),
            scratch((ROWS, PAD), BF16),
            scratch((ROWS, 128), F32),
            scratch((ROWS, 128), F32),
            scratch((16, 8, 128), F32),
            scratch((16, 8, 128), F32),
            scratch((NZ, 2, NV, 32, 256), BF16),
            scratch((NZ, 2, NV, 32, 256), BF16),
            scratch((NZ, 2, NV, 32, 256), F32),
            *[scratch((NZ, n, 32, 256), BF16) for n in halves],
            *[scratch((NZ, n, 32, 256), BF16) for n in halves],
            scratch((NZ, 32, 256), BF16),
            scratch((NZ, 32, 256), BF16),
            scratch((NV, 32, 256), BF16),
            scratch((NC * 128, HEAD), BF16),
            scratch((NC * 128, HEAD), BF16),
            scratch((NC * 64, HEAD), BF16),
            scratch((64, NC * 128), F32),
            scratch((NZ, 2, 2, 64, HEAD), F32),
            *[scratch((NZ, 2, 64, HEAD), BF16)] * 4,
            scratch((NZ, 2, 2, 64, HEAD), BF16),
            scratch((NZ, 2, 2, 8, 128), F32),
            scratch((128, 128), F32),
            scratch((128, NC * 64), F32),
            dma((8,)), dma((NZ,)), dma((NZ,)), dma((4, 15)), dma((4, 15)), dma((4, 16)), dma((4, 16)),
            dma((9,)), dma((9,)), dma((8,)), dma((8,)),
            dma((16,)), dma((16,)), dma((16,)), dma((16,)), dma((NZ,)), dma((NZ,)),
            dma((NZ, 4)), dma((NZ, 4)), dma((NZ,)), dma((NZ,)), dma((7,)), dma((7,)),
            dma, dma, dma((15,)), dma((15,)), dma((15,)), dma((15,)), dma((15,)), dma((15,)),
            dma((16,)), dma((16,)), dma((16,)), dma((16,)),
        ],
        compiler_params=pltpu.CompilerParams(
            collective_id=0, has_side_effects=True, vmem_limit_bytes=61 * 1024 * 1024
        ),
        name="step",
    )(*operands)


def emit_kernel(loss, resid_t, dq, dk, dv, loss_out, resid_out, dq_out, dk_out, dv_out):
    loss_out[0, 0] = loss[0, 0]
    resid_out[...] = resid_t[...]
    dq_out[...] = dq[...]
    dk_out[...] = dk[...]
    dv_out[...] = dv[...]


def emit(loss, *results):
    vmem = pl.BlockSpec(memory_space=pltpu.VMEM)
    return pl.pallas_call(
        emit_kernel,
        out_shape=(jax.ShapeDtypeStruct((1, 1), F32),)
        + tuple(jax.ShapeDtypeStruct(array.shape, array.dtype) for array in results),
        in_specs=[vmem] * 5,
        out_specs=(pl.BlockSpec(memory_space=pltpu.SMEM),) + (vmem,) * 4,
        name="emit",
    )(loss, *results)


def per_device(
    hidden,
    norm_gain,
    head_weight,
    targets,
    loss_rows,
    stretch_of_slot,
    queries,
    key_states,
    attention_values,
    output_weight,
):
    spans = stretch_of_slot.reshape(NC, 2)
    local = loss_rows.reshape(NC, LPD)
    place = jnp.where(local < 64, spans[:, 0:1], spans[:, 1:2]) * 64 + lax.rem(local, 64)
    query_pos = jnp.broadcast_to(place[:, None, :], (NC, 8, LPD)).reshape(1, NC * 64).astype(F32)
    key_pos = stretch_of_slot[:, None] * 64 + lax.broadcasted_iota(jnp.int32, (64, 64), 1)
    key_pos = key_pos.reshape(1, 4096).astype(F32)
    loss, resid_t, dq, dk, dv = step(
        hidden,
        queries,
        key_states,
        attention_values,
        loss_rows.astype(F32).reshape(1, ROWS),
        targets.reshape(1, ROWS),
        norm_gain.reshape(1, WIDTH),
        key_pos,
        query_pos,
        output_weight,
        head_weight,
    )
    loss, resid_t, dq, dk, dv = emit(loss, resid_t, dq, dk, dv)
    return (loss[0, 0], dq, dk, dv, resid_t)


def solution(mesh):
    placed = (
        P("ctx", "vocab"),
        P(),
        P(("vocab", "ctx"), None),
        P(),
        P(),
        P(),
        P("ctx", "vocab"),
        P("ctx", "vocab"),
        P("ctx", "vocab"),
        P("vocab", "ctx"),
    )
    return jax.shard_map(
        per_device,
        mesh=mesh,
        in_specs=placed,
        out_specs=(P(), P("ctx", "vocab"), P("ctx", "vocab"), P("ctx", "vocab"), P("ctx", None)),
        check_vma=False,
    )
```

```python
import functools

import jax
import jax.numpy as jnp
from jax import lax
from jax.experimental import pallas as pl
from jax.experimental.pallas import tpu as pltpu
from jax.sharding import PartitionSpec as P

MESH = pl.DeviceIdType.MESH
F32 = jnp.float32
BF16 = jnp.bfloat16

HEAD = 128
ROWS = 256
WIDTH = 8192
NV, NC, NZ = 8, 32, 8
LPD = 8
VOC = 594
PAD = 640
KVQ = 320
EPS = 1e-06
GRAD_WEIGHT = 16.0
SCALE = HEAD ** (-0.5)
FILL = -1e30

ORDERS = (
    (("x", 1), ("x", 3), ("y", 1), ("y", 3)),
    (("x", 3), ("x", 1), ("y", 3), ("y", 1)),
    (("y", 1), ("y", 3), ("x", 1), ("x", 3)),
    (("y", 3), ("y", 1), ("x", 3), ("x", 1)),
)

NEAR_FIRST = (0, 1, 7, 2, 6, 3, 5, 4)
FAR_FIRST = (4, 3, 5, 2, 6, 1, 7, 0)
COLOUR = {d: i % 4 for i, d in enumerate(NEAR_FIRST)}

GATHER = (
    ("z", 0), ("z", 3), ("z", 1), (0, 0), ("z", 2), ("r", 1), (3, 0), (1, 0), (0, 1), (2, 0), (3, 1), (1, 1), (0, 2),
    (2, 1), (3, 2), (1, 2), ("r", 2), (0, 3), (2, 2), (3, 3), ("p", 0), (1, 3), ("p", 3), (2, 3), ("p", 1), ("p", 2),
)


class Place:
    def __init__(self):
        self.v = lax.axis_index("vocab")
        self.c = lax.axis_index("ctx")
        self.xl = lax.div(self.v, 4)
        self.y = lax.rem(self.v, 4)
        self.z = lax.div(self.c, 4)
        self.xh = lax.rem(lax.div(self.c, 2), 2)
        self.core = lax.rem(self.c, 2)

    def y_off(self, off):
        y = self.y
        if off == 0:
            return y
        if off == 1:
            return y + 1 - 2 * lax.rem(y, 2)
        if off == 2:
            return lax.rem(y + 2, 4)
        return 3 - y

    def xl_off(self, off):
        return 1 - self.xl if off & 1 else self.xl

    def xh_off(self, off):
        return 1 - self.xh if off & 2 else self.xh

    def v_at(self, x_off=0, y_off=0):
        return self.xl_off(x_off) * 4 + self.y_off(y_off)

    def dev(self, x_off=0, y_off=0, z=None, core_off=0):
        z = self.z if z is None else z
        core = 1 - self.core if core_off else self.core
        return (self.v_at(x_off, y_off), z * 4 + self.xh_off(x_off) * 2 + core)

    def z_plus(self, d):
        return lax.rem(self.z + d + NZ, NZ)


def greet(devices):
    barrier = pltpu.get_barrier_semaphore()
    for device in devices:
        pl.semaphore_signal(barrier, inc=1, device_id=device, device_id_type=MESH)
    return functools.partial(pl.semaphore_wait, barrier, len(devices))


def remote(src, dst, send, recv, device):
    copy = pltpu.make_async_remote_copy(
        src_ref=src, dst_ref=dst, send_sem=send, recv_sem=recv, device_id=device, device_id_type=MESH
    )
    copy.start()
    return copy


def offsets(order, done):
    held = [(0, 0)]
    for axis, mask in order[:done]:
        held = held + [(ox ^ mask, oy) if axis == "x" else (ox, oy ^ mask) for ox, oy in held]
    return held


def pieces(me, order, step):
    every = slice(None)
    if step < 0:
        return [(me.xh, me.xl, me.y)]
    axis, mask = order[step]
    second = step in (1, 3)
    first_mask = order[step - 1][1] if second else 0
    other = step >= 2
    if axis == "x":
        y = every if other else me.y
        if not second:
            return [(me.xh_off(mask), me.xl_off(mask), y)]
        if first_mask == 1:
            return [(me.xh_off(mask), every, y)]
        return [(me.xh_off(m), me.xl_off(m), y) for m in (mask, mask ^ first_mask)]
    xh, xl = (every, every) if other else (me.xh, me.xl)
    if not second:
        return [(xh, xl, me.y_off(mask))]
    if first_mask == 1:
        return [(xh, xl, pl.ds(2 - 2 * lax.div(me.y, 2), 2))]
    return [(xh, xl, me.y_off(m)) for m in (mask, mask ^ first_mask)]


def partner(me, axis, mask):
    return me.dev(x_off=mask) if axis == "x" else me.dev(y_off=mask)


def column(row_vector, width=128):
    return jnp.transpose(jnp.broadcast_to(row_vector, (width, row_vector.shape[1])))


def merge(parts):
    top = jnp.max(parts[:, 0:2], axis=0)
    weight = jnp.exp(parts[:, 0:2] - top[None])
    total = jnp.sum(parts[:, 2:4] * weight, axis=0)
    first = jnp.sum(parts[:, 4:6] * weight, axis=0)
    hit = jnp.sum(parts[:, 6:8], axis=0)
    return jnp.concatenate([top, total, first, hit], axis=0)


def wide(two):
    return jnp.concatenate([two[0:1], two[1:2]], axis=1)


def step_kernel(
    hidden_hbm, queries_hbm, keys_hbm, values_hbm, lrows_hbm, targets_hbm, gain_hbm, stretch_hbm, out_hbm, weight_hbm,
    loss, resid_t, dq, dk, dv,
    weight, rows, y, kvq, logits, grad_t, rms_col, inner_col, st1, st2, cs, cr, acc,
    sb1, sb2, sb3, sb4, rb1, rb2, rb3, rb4, zs, zr, resid,
    k_all, v_all, q_all, probs, part, pc, pr, rs, rx, rz, rr, grads, extras, square_tile, s2,
    key_pos, query_pos, gain, out_weight, hidden, queries, lrows_in, targets_in, gain_in, stretch, w_sem, o_sem, i_sem, z_s, z_r, a_s, a_r, f_s, f_r, k_s, k_r, kf_s, kf_r, s1_s, s1_r, s2_s, s2_r,
    c_s, c_r, x_s, x_r, t_s, t_r, v_s, v_r, pc_s, pc_r, rx_s, rx_r, r_s, r_r, g_s, g_r, e_s, e_r, gx_s, gx_r, fg_s, fg_r, ex_s, ex_r, fe_s, fe_r,
):
    me = Place()
    mate = me.dev(core_off=1)
    group1 = [(d, o) for d in range(NZ) for o in range(2) if (d, o) != (0, 0)]
    group2 = [(ox, oy) for ox in range(4) for oy in range(4) if (ox, oy) != (0, 0)]
    arrivals = []
    for i, (src, dst) in enumerate([
        (lrows_hbm, lrows_in), (hidden_hbm, hidden), (queries_hbm, queries),
        (keys_hbm, kvq.at[me.z, me.xh, me.core, 0:128]), (values_hbm, kvq.at[me.z, me.xh, me.core, 128:256]),
        (targets_hbm, targets_in), (gain_hbm, gain_in), (stretch_hbm, stretch),
    ]):
        arrival = pltpu.make_async_copy(src, dst, i_sem.at[i])
        arrival.start()
        arrivals.append(arrival)
    greeted = greet(
        [me.dev(z=me.z_plus(d), core_off=o) for d, o in group1]
        + [me.dev(ox, oy) for ox, oy in group2]
    )
    loads = []
    for j in range(8):
        section = (slice(None), slice(1024 * j, 1024 * j + 1024))
        load = pltpu.make_async_copy(weight_hbm.at[section], weight.at[section], w_sem.at[j])
        load.start()
        loads.append(load)
    out_load = pltpu.make_async_copy(out_hbm, out_weight, o_sem)
    out_load.start()
    started = []

    def go(*args):
        copy = remote(*args)
        started.append(copy)
        return copy

    for arrival in arrivals:
        arrival.wait()
    lane = lax.broadcasted_iota(jnp.int32, (LPD, ROWS), 1)
    line = lax.broadcasted_iota(jnp.int32, (LPD, ROWS), 0)
    lrows = wide(lrows_in[...]).astype(F32)
    own = jnp.sum(jnp.where(lane == me.c * LPD + line, lrows, 0.0), axis=1, keepdims=True)
    rows_at = lax.broadcasted_iota(jnp.int32, (LPD, 128), 1).astype(F32)
    pick = (own == rows_at).astype(F32).astype(BF16)
    rows[0, me.xh, me.core, me.xl, me.y] = jnp.dot(pick, hidden[...], preferred_element_type=F32).astype(BF16)
    picked_q = jnp.dot(pick, queries[...], preferred_element_type=F32).astype(BF16)
    for head in range(8):
        kvq[me.z, me.xh, me.core, 256 + 8 * head : 264 + 8 * head, :] = picked_q[:, 128 * head : 128 * head + 128]
    greeted()

    def piece(k, at):
        xh, xl, y = at
        return rows.at[pl.ds(2 * k, 2), xh, me.core, xl, y]

    z_copies = {}
    for d in FAR_FIRST[:-1]:
        back = NZ - d
        z_copies[back] = go(
            rows.at[0, me.xh, me.core, me.xl, me.y], rows.at[back, me.xh, me.core, me.xl, me.y],
            z_s.at[d], z_r.at[back], me.dev(z=me.z_plus(d)),
        )
    own_kvq = kvq.at[me.z, me.xh, me.core]
    k_x = go(own_kvq, own_kvq, k_s.at[0], k_r.at[0], me.dev(x_off=2))

    a_copies, f_copies, kf_copies, ring = {}, {}, [], {}

    def spread(k, step):
        order = ORDERS[k]
        for j, at in enumerate(pieces(me, order, step)):
            here = piece(k, at)
            for later in range(step + 1, 4):
                a_copies.setdefault((k, later), []).append(
                    go(
                        here, here, a_s.at[k, later, 2 * step + 2 + j], a_r.at[k, later, 2 * step + 2 + j],
                        partner(me, *order[later]),
                    )
                )
            f_copies.setdefault(k, []).append(
                go(here, here, f_s.at[k, 2 * step + 2 + j], f_r.at[k, 2 * step + 2 + j], mate)
            )

    def place_tables():
        spans = jnp.broadcast_to(stretch[...].astype(F32), (8, 64)).astype(BF16)

        def spread_spans(slot, width):
            hot = lax.broadcasted_iota(jnp.int32, (64, width), 0) == slot
            return jnp.dot(spans, hot.astype(F32).astype(BF16), preferred_element_type=F32)[0:1]

        at = lax.broadcasted_iota(jnp.int32, (1, NC * 128), 1)
        base = spread_spans(lax.shift_right_logical(at, 6), NC * 128)
        key_pos[...] = base * 64.0 + (at & 63).astype(F32)
        at = lax.broadcasted_iota(jnp.int32, (1, NC * 64), 1)
        owner = lax.shift_right_logical(at, 6)
        hot = lax.broadcasted_iota(jnp.int32, (ROWS, NC * 64), 0) == owner * LPD + (at & 7)
        local = jnp.dot(
            jnp.broadcast_to(lrows, (8, ROWS)).astype(BF16), hot.astype(F32).astype(BF16), preferred_element_type=F32
        )[0:1]
        first, second = spread_spans(owner * 2, NC * 64), spread_spans(owner * 2 + 1, NC * 64)
        query_pos[...] = jnp.where(local < 64.0, first * 64.0 + local, second * 64.0 + (local - 64.0))
        for t in range(WIDTH // 128):
            gain[:, 128 * t : 128 * t + 128] = gain_in[t : t + 1, :]

    def ring_step(step):
        lo, hi = (0, KVQ) if step < 4 else (0, 160)
        lo2, hi2 = (0, KVQ) if step < 4 else (160, KVQ)
        up, down = me.z_plus(-(step - 1)), me.z_plus(step - 1)
        right = kvq.at[up, :, me.core, lo:hi]
        left = kvq.at[down, :, me.core, lo2:hi2]
        ring[step] = (
            go(right, right, k_s.at[2 * step - 1], k_r.at[2 * step - 1], me.dev(z=me.z_plus(1))),
            go(left, left, k_s.at[2 * step], k_r.at[2 * step], me.dev(z=me.z_plus(-1))),
        )

    def ring_forward(slot, z):
        here = kvq.at[z, :, me.core]
        kf_copies.append(go(here, here, kf_s.at[slot], kf_r.at[slot], mate))

    def ring_wait(step):
        ring[step][0].wait_recv()
        if step < 4:
            ring_forward(2 * step - 1, me.z_plus(-step))
        ring[step][1].wait_recv()
        ring_forward(2 * step if step < 4 else 7, me.z_plus(step))

    def prepare(d, _):
        lines = pl.ds(pl.multiple_of(lax.rem(me.z + d, NZ) * 32, 32), 32)
        square = jnp.zeros((32, 128), F32)
        for v in range(NV):
            cols = slice(1024 * v, 1024 * v + 1024)
            x = rows[d, :, :, v // 4, v % 4].astype(F32).reshape(32, 1024)
            y[lines, cols] = (x * gain[:, cols]).astype(BF16)
            sq = x * x
            for t in range(8):
                square = square + sq[:, 128 * t : 128 * t + 128]
        inv = lax.rsqrt(jnp.sum(square, axis=1, keepdims=True) * (1.0 / WIDTH) + EPS)
        rms_col[lines, :] = jnp.broadcast_to(inv, (32, 128))
        return 0

    place_tables()
    for kind, which in GATHER:
        if kind == "z":
            for d in (2 * which, 2 * which + 1):
                if d:
                    z_copies[d].wait_recv()
            spread(which, -1)
        elif kind == "r":
            if which == 1:
                k_x.wait_recv()
                ring_forward(0, me.z)
            else:
                ring_wait(which - 1)
            ring_step(which)
        elif kind == "p":
            for copy in f_copies[which]:
                copy.wait_recv()
            lax.fori_loop(2 * which, 2 * which + 2, prepare, 0)
        else:
            for copy in a_copies[kind, which]:
                copy.wait_recv()
            spread(kind, which)
    ring_wait(2)
    ring_step(3)

    inv_row = jnp.transpose(rms_col[...])[0:1, :]

    logits[PAD - 48 : PAD, :] = jnp.zeros((48, ROWS), F32)
    for j in range(8):
        loads[j].wait()
        term = lax.dot_general(
            weight[:, 1024 * j : 1024 * j + 1024], y[:, 1024 * j : 1024 * j + 1024],
            (((1,), (1,)), ((), ())), preferred_element_type=F32,
        )
        logits[0:VOC, :] = term if j == 0 else logits[0:VOC, :] + term
        if j == 6:
            ring_wait(3)
            ring_step(4)

    ids = lax.broadcasted_iota(jnp.int32, (PAD, ROWS), 0)
    real = ids < VOC
    first_id = (me.v * NC + me.c) * VOC
    is_target = ((ids + first_id) == wide(targets_in[...])) & real
    value = jnp.where(real, logits[...] * inv_row, FILL)
    logits[...] = value
    top = jnp.max(value, axis=0, keepdims=True)
    raw = jnp.exp(value - top)
    stats = (
        top,
        jnp.sum(raw, axis=0, keepdims=True),
        jnp.sum(raw * value, axis=0, keepdims=True),
        jnp.sum(jnp.where(is_target, value, 0.0), axis=0, keepdims=True),
    )
    packed = jnp.concatenate([piece[:, h : h + 128] for piece in stats for h in (0, 128)], axis=0)
    slot1 = me.z * 2 + me.core
    st1[slot1] = packed
    waits = []
    for i, (d, o) in enumerate(group1):
        waits.append(
            go(st1.at[slot1], st1.at[slot1], s1_s.at[i], s1_r.at[2 * d + o], me.dev(z=me.z_plus(d), core_off=o))
        )
    for copy in waits:
        copy.wait_recv()
    slot2 = (me.xh * 2 + me.xl) * 4 + me.y
    st2[slot2] = merge(st1[...])
    waits = []
    for i, (ox, oy) in enumerate(group2):
        waits.append(go(st2.at[slot2], st2.at[slot2], s2_s.at[i], s2_r.at[4 * ox + oy], me.dev(ox, oy)))
    ring_wait(4)
    for copy in kf_copies:
        copy.wait_recv()

    k_all[...] = kvq[:, :, :, 0:128, :].reshape(NC * 128, HEAD)
    v_all[...] = kvq[:, :, :, 128:256, :].reshape(NC * 128, HEAD)
    q_all[...] = kvq[:, :, :, 256:320, :].reshape(NC * 64, HEAD)
    q_own = kvq[me.z, me.xh, me.core, 256:320, :]
    lane = lax.broadcasted_iota(jnp.int32, (64, NC * 64), 1)
    line = lax.broadcasted_iota(jnp.int32, (64, NC * 64), 0)
    query_col = jnp.sum(jnp.where(lane == me.c * 64 + line, query_pos[...], 0.0), axis=1, keepdims=True)
    scores = lax.dot_general(q_own, k_all[...], (((1,), (1,)), ((), ())), preferred_element_type=F32)
    seen = key_pos[...] <= query_col
    masked = jnp.where(seen, scores * SCALE, FILL)
    top = jnp.max(masked, axis=1, keepdims=True)
    raw = jnp.where(seen, jnp.exp(masked - top), 0.0)
    total = jnp.sum(raw, axis=1, keepdims=True)
    probs[...] = raw / total
    row_log_total = top + jnp.log(total)

    for copy in waits:
        copy.wait_recv()
    final = merge(st2[...])
    log_total = wide(final[0:2] + jnp.log(final[2:4]))
    hit = wide(final[6:8])
    grad = GRAD_WEIGHT * (jnp.exp(logits[...] - log_total) - is_target.astype(F32))
    grad_t[...] = jnp.transpose(grad).astype(BF16)

    def chunk(z, xh, core):
        cols = pl.ds(pl.multiple_of((z * 4 + xh * 2 + core) * 256, 256), 256)
        return jnp.dot(grad_t[:, 0:VOC], weight[:, cols], preferred_element_type=F32).reshape(NV, 32, 256)

    c_copies = {}

    def give(d):
        z = me.z_plus(d)

        def other(xh, _):
            cs[z, xh] = chunk(z, xh, 1 - me.core).astype(BF16)
            return 0

        lax.fori_loop(0, 2, other, 0)
        c_copies[d] = go(cs.at[z], cr.at[z], c_s.at[d], c_r.at[d], mate)

    def keep_own(d):
        z = me.z_plus(d)

        def mine(xh, _):
            acc[z, xh] = chunk(z, xh, me.core)
            return 0

        lax.fori_loop(0, 2, mine, 0)

    sends, recvs = (sb1, sb2, sb3, sb4), (rb1, rb2, rb3, rb4)
    moving = {}

    def at(d, off):
        return (me.z_plus(d), me.xh_off(off[0]), me.v_at(*off))

    def halve(d, step):
        back = ORDERS[COLOUR[d]]
        axis, mask = back[3 - step]
        keep, before = offsets(back, 3 - step), offsets(back, 4 - step)
        for off in before:
            here = at(d, off)
            if step == 0:
                extra = cr[here].astype(F32)
            else:
                extra = recvs[step - 1][d, before.index(off)].astype(F32)
            summed = acc[here] + extra
            away = (off[0] ^ mask, off[1]) if axis == "x" else (off[0], off[1] ^ mask)
            if away in keep:
                sends[step][d, keep.index(away)] = summed.astype(BF16)
            else:
                acc[here] = summed
        moving[d, step] = go(
            sends[step].at[d], recvs[step].at[d], x_s.at[d, step], x_r.at[d, step], partner(me, axis, mask)
        )

    z_copies = []
    lag = 4
    give(FAR_FIRST[0])
    for i in range(NZ + 4 * lag):
        if i + 1 < NZ:
            give(FAR_FIRST[i + 1])
        if i < NZ:
            d = FAR_FIRST[i]
            keep_own(d)
            c_copies[d].wait_recv()
            halve(d, 0)
        for step in range(1, 5):
            if not 0 <= i - lag * step < NZ:
                continue
            d = FAR_FIRST[i - lag * step]
            moving[d, step - 1].wait_recv()
            if step < 4:
                halve(d, step)
                continue
            zs[d] = (acc[at(d, (0, 0))] + rb4[d, 0].astype(F32)).astype(BF16)
            if d:
                z_copies.append(go(zs.at[d], zr.at[me.z], t_s.at[d], t_r.at[d], me.dev(z=me.z_plus(d))))
            else:
                zr[me.z] = zs[d]

    loss[...] = jnp.broadcast_to(jnp.mean(log_total - hit, axis=1, keepdims=True), (8, 128))
    inner_col[...] = column((wide(final[4:6] / final[2:4]) - hit) * (GRAD_WEIGHT / WIDTH))
    k_own = kvq[me.z, me.xh, me.core, 0:128, :]
    v_own = kvq[me.z, me.xh, me.core, 128:256, :]
    s2[...] = lax.dot_general(k_own, q_all[...], (((1,), (1,)), ((), ())), preferred_element_type=F32)
    for copy in z_copies:
        copy.wait_recv()
    normed_grad = jnp.sum(zr[...].astype(F32), axis=0)
    cols = pl.ds(pl.multiple_of(me.c * 256, 256), 256)
    lines = pl.ds(pl.multiple_of(me.v * 32, 32), 32)
    inv = rms_col[lines, 0:1]
    inside = pl.ds(pl.multiple_of(lax.rem(me.c, 4) * 256, 256), 256)
    apart = lax.rem(me.v - me.z + NZ, NZ)
    picked = rows[apart, :, :, lax.div(me.z, 4), lax.rem(me.z, 4), :, inside].astype(F32).reshape(32, 256)
    out = inv * (normed_grad * gain[:, cols] - picked * (inv * inner_col[lines, 0:1]))
    resid[me.v] = out.astype(BF16)
    v_copies = []
    for i, (ox, oy) in enumerate([(o, q) for o in range(2) for q in range(4) if (o, q) != (0, 0)]):
        v_copies.append(go(resid.at[me.v], resid.at[me.v], v_s.at[i], v_r.at[i], me.dev(ox, oy)))
    high = probs[...].astype(BF16)
    low = (probs[...] - high.astype(F32)).astype(BF16)
    attn_out = jnp.dot(high, v_all[...], preferred_element_type=F32) + jnp.dot(
        low, v_all[...], preferred_element_type=F32
    )
    for copy in v_copies:
        copy.wait_recv()

    out_load.wait()
    wide_part = lax.dot_general(
        resid[...].reshape(ROWS, 256), out_weight[...], (((1,), (1,)), ((), ())), preferred_element_type=F32
    )
    for h in range(8):
        part[:, :, :, 8 * h : 8 * h + 8, :] = wide_part[:, 128 * h : 128 * h + 128].reshape(NZ, 2, 2, LPD, HEAD)
    pc_copies = {}
    for d in FAR_FIRST:
        z = me.z_plus(d)
        pc[z] = part[z, :, 1 - me.core].astype(BF16)
        pc_copies[d] = go(pc.at[z], pr.at[z], pc_s.at[d], pc_r.at[d], mate)
    x_copies, r_copies = {}, []
    for d in FAR_FIRST:
        z = me.z_plus(d)
        pc_copies[d].wait_recv()
        there = 1 - me.xh
        rs[z] = (part[z, there, me.core] + pr[z, there].astype(F32)).astype(BF16)
        x_copies[d] = go(rs.at[z], rx.at[z], rx_s.at[d], rx_r.at[d], me.dev(x_off=2))
    for d in FAR_FIRST:
        z = me.z_plus(d)
        x_copies[d].wait_recv()
        mine = part[z, me.xh, me.core] + pr[z, me.xh].astype(F32) + rx[z].astype(F32)
        if d:
            rz[z] = mine.astype(BF16)
            r_copies.append(go(rz.at[z], rr.at[me.z], r_s.at[d], r_r.at[d], me.dev(z=z)))
        else:
            rr[me.z] = mine.astype(BF16)
    resid_t[...] = jnp.transpose(resid[...].astype(F32).reshape(ROWS, 256)).astype(BF16)
    for copy in r_copies:
        copy.wait_recv()
    grad_own = jnp.sum(rr[...].astype(F32), axis=0).astype(BF16)
    grads[me.z, me.xh, me.core] = grad_own
    own_g, own_e = grads.at[me.z, me.xh, me.core], extras.at[me.z, me.xh, me.core]

    def hand_out(own, send, recv):
        return {d: go(own, own, send.at[d], recv.at[d], me.dev(z=me.z_plus(d))) for d in FAR_FIRST[:-1]}

    g_copies = hand_out(own_g, g_s, g_r)
    delta = jnp.sum(grad_own.astype(F32) * attn_out, axis=1, keepdims=True)
    lane = lax.broadcasted_iota(jnp.int32, (64, 128), 1)
    square_tile[...] = jnp.zeros((128, 128), F32)
    square_tile[0:64, :] = jnp.where(lane == 0, delta, jnp.where(lane == 1, row_log_total, 0.0))
    extras[me.z, me.xh, me.core] = jnp.transpose(square_tile[...])[0:8, :]
    e_copies = hand_out(own_e, e_s, e_r)
    side = me.dev(x_off=2)
    forwards, sides = [], {}

    def hand_on(d, xh, slot):
        here = grads.at[me.z_plus(-d), xh, me.core]
        if not slot:
            sides[d] = go(here, here, gx_s.at[d], gx_r.at[d], side)
        forwards.append(go(here, here, fg_s.at[slot, d], fg_r.at[slot, d], mate))

    hand_on(0, me.xh, 0)
    prob_grad = lax.dot_general(grad_own, v_all[...], (((1,), (1,)), ((), ())), preferred_element_type=F32)
    score_grad = (probs[...] * (prob_grad - delta)).astype(BF16)
    query_grad = jnp.dot(score_grad, k_all[...], preferred_element_type=F32) * SCALE
    for h in range(8):
        dq[:, 128 * h : 128 * h + 128] = query_grad[8 * h : 8 * h + 8, :].astype(BF16)
    for d in NEAR_FIRST[1:]:
        g_copies[d].wait_recv()
        hand_on(d, me.xh, 0)
    for copy in e_copies.values():
        copy.wait_recv()
    line_e = extras.at[:, me.xh, me.core]
    e_side = go(line_e, line_e, ex_s, ex_r, side)
    for d in NEAR_FIRST:
        sides[d].wait_recv()
        hand_on(d, 1 - me.xh, 1)
    e_side.wait_recv()
    all_e = extras.at[:, :, me.core]
    forwards.append(go(all_e, all_e, fe_s, fe_r, mate))
    own_key_pos = key_pos[:, pl.ds(pl.multiple_of(me.c * 128, 128), 128)]
    lane = lax.broadcasted_iota(jnp.int32, (128, 128), 1)
    line = lax.broadcasted_iota(jnp.int32, (128, 128), 0)
    key_col = jnp.sum(jnp.where(lane == line, own_key_pos, 0.0), axis=1, keepdims=True)
    seen2 = key_col <= query_pos[...]
    for copy in forwards:
        copy.wait_recv()
    grads_all = grads[...].reshape(NC * 64, HEAD)
    e_all = extras[...].reshape(NC, 8, 128)
    delta_all = jnp.concatenate([e_all[i, 0:1, 0:64] for i in range(NC)], axis=1)
    log_all = jnp.concatenate([e_all[i, 1:2, 0:64] for i in range(NC)], axis=1)
    probs2 = jnp.where(seen2, jnp.exp(s2[...] * SCALE - log_all), 0.0)
    dv[...] = jnp.dot(probs2.astype(BF16), grads_all, preferred_element_type=F32).astype(BF16)
    prob_grad2 = lax.dot_general(v_own, grads_all, (((1,), (1,)), ((), ())), preferred_element_type=F32)
    score_grad2 = (probs2 * (prob_grad2 - delta_all)).astype(BF16)
    dk[...] = (jnp.dot(score_grad2, q_all[...], preferred_element_type=F32) * SCALE).astype(BF16)
    for copy in started:
        copy.wait_send()


def step(*operands):
    vmem = pl.BlockSpec(memory_space=pltpu.VMEM)
    dma = pltpu.SemaphoreType.DMA
    scratch = pltpu.VMEM
    halves = [8, 4, 2, 1]
    return pl.pallas_call(
        step_kernel,
        out_shape=(
            jax.ShapeDtypeStruct((8, 128), F32),
            jax.ShapeDtypeStruct((256, ROWS), BF16),
            jax.ShapeDtypeStruct((LPD, 1024), BF16),
            jax.ShapeDtypeStruct((128, HEAD), BF16),
            jax.ShapeDtypeStruct((128, HEAD), BF16),
        ),
        in_specs=[pl.BlockSpec(memory_space=pl.ANY)] * 10,
        out_specs=(vmem,) * 5,
        scratch_shapes=[
            scratch((VOC, WIDTH), BF16),
            scratch((NZ, 2, 2, 2, 4, LPD, 1024), BF16),
            scratch((ROWS, WIDTH), BF16),
            scratch((NZ, 2, 2, KVQ, HEAD), BF16),
            scratch((PAD, ROWS), F32),
            scratch((ROWS, PAD), BF16),
            scratch((ROWS, 128), F32),
            scratch((ROWS, 128), F32),
            scratch((16, 8, 128), F32),
            scratch((16, 8, 128), F32),
            scratch((NZ, 2, NV, 32, 256), BF16),
            scratch((NZ, 2, NV, 32, 256), BF16),
            scratch((NZ, 2, NV, 32, 256), F32),
            *[scratch((NZ, n, 32, 256), BF16) for n in halves],
            *[scratch((NZ, n, 32, 256), BF16) for n in halves],
            scratch((NZ, 32, 256), BF16),
            scratch((NZ, 32, 256), BF16),
            scratch((NV, 32, 256), BF16),
            scratch((NC * 128, HEAD), BF16),
            scratch((NC * 128, HEAD), BF16),
            scratch((NC * 64, HEAD), BF16),
            scratch((64, NC * 128), F32),
            scratch((NZ, 2, 2, 64, HEAD), F32),
            *[scratch((NZ, 2, 64, HEAD), BF16)] * 2,
            *[scratch((NZ, 64, HEAD), BF16)] * 4,
            scratch((NZ, 2, 2, 64, HEAD), BF16),
            scratch((NZ, 2, 2, 8, 128), F32),
            scratch((128, 128), F32),
            scratch((128, NC * 64), F32),
            scratch((1, NC * 128), F32),
            scratch((1, NC * 64), F32),
            scratch((1, WIDTH), F32),
            scratch((1024, 256), BF16),
            scratch((128, 1024), BF16),
            scratch((128, 1024), BF16),
            scratch((2, 128), jnp.int32),
            scratch((2, 128), jnp.int32),
            scratch((64, 128), F32),
            scratch((1, 64), jnp.int32),
            dma((8,)), dma, dma((8,)), dma((NZ,)), dma((NZ,)),
            dma((4, 4, 8)), dma((4, 4, 8)), dma((4, 10)), dma((4, 10)),
            dma((9,)), dma((9,)), dma((8,)), dma((8,)),
            dma((16,)), dma((16,)), dma((16,)), dma((16,)), dma((NZ,)), dma((NZ,)),
            dma((NZ, 4)), dma((NZ, 4)), dma((NZ,)), dma((NZ,)), dma((7,)), dma((7,)),
            *[dma((NZ,))] * 12, dma((2, NZ)), dma((2, NZ)), dma, dma, dma, dma,
        ],
        compiler_params=pltpu.CompilerParams(
            collective_id=0, has_side_effects=True, vmem_limit_bytes=61 * 1024 * 1024
        ),
        name="step",
    )(*operands)


def emit_kernel(loss, resid_t, dq, dk, dv, loss_out, resid_out, dq_out, dk_out, dv_out):
    loss_out[0, 0] = loss[0, 0]
    resid_out[...] = resid_t[...]
    dq_out[...] = dq[...]
    dk_out[...] = dk[...]
    dv_out[...] = dv[...]


def emit(loss, *results):
    vmem = pl.BlockSpec(memory_space=pltpu.VMEM)
    return pl.pallas_call(
        emit_kernel,
        out_shape=(jax.ShapeDtypeStruct((1, 1), F32),)
        + tuple(jax.ShapeDtypeStruct(array.shape, array.dtype) for array in results),
        in_specs=[vmem] * 5,
        out_specs=(pl.BlockSpec(memory_space=pltpu.SMEM),) + (vmem,) * 4,
        name="emit",
    )(loss, *results)


def per_device(
    hidden,
    norm_gain,
    head_weight,
    targets,
    loss_rows,
    stretch_of_slot,
    queries,
    key_states,
    attention_values,
    output_weight,
):
    loss, resid_t, dq, dk, dv = step(
        hidden,
        queries,
        key_states,
        attention_values,
        loss_rows.reshape(2, 128),
        targets.reshape(2, 128),
        norm_gain.reshape(64, 128),
        stretch_of_slot.reshape(1, 64),
        output_weight,
        head_weight,
    )
    loss, resid_t, dq, dk, dv = emit(loss, resid_t, dq, dk, dv)
    return (loss[0, 0], dq, dk, dv, resid_t)


def solution(mesh):
    placed = (
        P("ctx", "vocab"),
        P(),
        P(("vocab", "ctx"), None),
        P(),
        P(),
        P(),
        P("ctx", "vocab"),
        P("ctx", "vocab"),
        P("ctx", "vocab"),
        P("vocab", "ctx"),
    )
    return jax.shard_map(
        per_device,
        mesh=mesh,
        in_specs=placed,
        out_specs=(P(), P("ctx", "vocab"), P("ctx", "vocab"), P("ctx", "vocab"), P("ctx", None)),
        check_vma=False,
    )
```

```python
import functools

import jax
import jax.numpy as jnp
from jax import lax
from jax.experimental import pallas as pl
from jax.experimental.pallas import tpu as pltpu
from jax.sharding import PartitionSpec as P

MESH = pl.DeviceIdType.MESH
F32 = jnp.float32
BF16 = jnp.bfloat16

HEAD = 128
ROWS = 256
WIDTH = 8192
NV, NC, NZ = 8, 32, 8
LPD = 8
VOC = 594
PAD = 640
KVQ = 320
EPS = 1e-06
GRAD_WEIGHT = 16.0
SCALE = HEAD ** (-0.5)
FILL = -1e30

ORDERS = (
    (("x", 1), ("x", 3), ("y", 1), ("y", 3)),
    (("x", 3), ("x", 1), ("y", 3), ("y", 1)),
    (("y", 1), ("y", 3), ("x", 1), ("x", 3)),
    (("y", 3), ("y", 1), ("x", 3), ("x", 1)),
)

NEAR_FIRST = (0, 1, 7, 2, 6, 3, 5, 4)
FAR_FIRST = (4, 3, 5, 2, 6, 1, 7, 0)
COLOUR = {d: i % 4 for i, d in enumerate(NEAR_FIRST)}

GATHER = (
    ("z", 0), ("z", 3), ("z", 1), (0, 0), ("z", 2), ("r", 1), (3, 0), (1, 0), (0, 1), (2, 0), (3, 1), (1, 1), (0, 2),
    (2, 1), (3, 2), (1, 2), ("r", 2), (0, 3), (2, 2), (3, 3), ("p", 0), (1, 3), ("p", 3), (2, 3), ("p", 1), ("p", 2),
)


class Place:
    def __init__(self):
        self.v = lax.axis_index("vocab")
        self.c = lax.axis_index("ctx")
        self.xl = lax.div(self.v, 4)
        self.y = lax.rem(self.v, 4)
        self.z = lax.div(self.c, 4)
        self.xh = lax.rem(lax.div(self.c, 2), 2)
        self.core = lax.rem(self.c, 2)

    def y_off(self, off):
        y = self.y
        if off == 0:
            return y
        if off == 1:
            return y + 1 - 2 * lax.rem(y, 2)
        if off == 2:
            return lax.rem(y + 2, 4)
        return 3 - y

    def xl_off(self, off):
        return 1 - self.xl if off & 1 else self.xl

    def xh_off(self, off):
        return 1 - self.xh if off & 2 else self.xh

    def v_at(self, x_off=0, y_off=0):
        return self.xl_off(x_off) * 4 + self.y_off(y_off)

    def dev(self, x_off=0, y_off=0, z=None, core_off=0):
        z = self.z if z is None else z
        core = 1 - self.core if core_off else self.core
        return (self.v_at(x_off, y_off), z * 4 + self.xh_off(x_off) * 2 + core)

    def z_plus(self, d):
        return lax.rem(self.z + d + NZ, NZ)


def greet(devices):
    barrier = pltpu.get_barrier_semaphore()
    for device in devices:
        pl.semaphore_signal(barrier, inc=1, device_id=device, device_id_type=MESH)
    return functools.partial(pl.semaphore_wait, barrier, len(devices))


def remote(src, dst, send, recv, device):
    copy = pltpu.make_async_remote_copy(
        src_ref=src, dst_ref=dst, send_sem=send, recv_sem=recv, device_id=device, device_id_type=MESH
    )
    copy.start()
    return copy


def offsets(order, done):
    held = [(0, 0)]
    for axis, mask in order[:done]:
        held = held + [(ox ^ mask, oy) if axis == "x" else (ox, oy ^ mask) for ox, oy in held]
    return held


def pieces(me, order, step):
    every = slice(None)
    if step < 0:
        return [(me.xh, me.xl, me.y)]
    axis, mask = order[step]
    second = step in (1, 3)
    first_mask = order[step - 1][1] if second else 0
    other = step >= 2
    if axis == "x":
        y = every if other else me.y
        if not second:
            return [(me.xh_off(mask), me.xl_off(mask), y)]
        if first_mask == 1:
            return [(me.xh_off(mask), every, y)]
        return [(me.xh_off(m), me.xl_off(m), y) for m in (mask, mask ^ first_mask)]
    xh, xl = (every, every) if other else (me.xh, me.xl)
    if not second:
        return [(xh, xl, me.y_off(mask))]
    if first_mask == 1:
        return [(xh, xl, pl.ds(2 - 2 * lax.div(me.y, 2), 2))]
    return [(xh, xl, me.y_off(m)) for m in (mask, mask ^ first_mask)]


def partner(me, axis, mask):
    return me.dev(x_off=mask) if axis == "x" else me.dev(y_off=mask)


def column(row_vector, width=128):
    return jnp.transpose(jnp.broadcast_to(row_vector, (width, row_vector.shape[1])))


def merge(parts):
    top = jnp.max(parts[:, 0:2], axis=0)
    weight = jnp.exp(parts[:, 0:2] - top[None])
    total = jnp.sum(parts[:, 2:4] * weight, axis=0)
    first = jnp.sum(parts[:, 4:6] * weight, axis=0)
    hit = jnp.sum(parts[:, 6:8], axis=0)
    return jnp.concatenate([top, total, first, hit], axis=0)


def wide(two):
    return jnp.concatenate([two[0:1], two[1:2]], axis=1)


def step_kernel(
    hidden_hbm, queries_hbm, keys_hbm, values_hbm, lrows_hbm, targets_hbm, gain_hbm, stretch_hbm, out_hbm, weight_hbm,
    loss, resid_t, dq, dk, dv,
    weight, rows, y, kvq, logits, logits_t, target_t, grad_t, rms_col, inner_col, st1, st2, cs, cr, acc,
    sb1, sb2, sb3, sb4, rb1, rb2, rb3, rb4, zs, zr, resid,
    k_all, v_all, q_all, probs, part, pc, pr, rs, rx, rz, rr, grads, extras, square_tile, s2,
    key_pos, query_pos, gain, out_weight, hidden, queries, lrows_in, targets_in, gain_in, stretch, w_sem, o_sem, i_sem, z_s, z_r, a_s, a_r, f_s, f_r, k_s, k_r, kf_s, kf_r, s1_s, s1_r, s2_s, s2_r,
    c_s, c_r, x_s, x_r, t_s, t_r, v_s, v_r, pc_s, pc_r, rx_s, rx_r, r_s, r_r, g_s, g_r, e_s, e_r, gx_s, gx_r, fg_s, fg_r, ex_s, ex_r, fe_s, fe_r,
):
    me = Place()
    mate = me.dev(core_off=1)
    group1 = [(d, o) for d in range(NZ) for o in range(2) if (d, o) != (0, 0)]
    group2 = [(ox, oy) for ox in range(4) for oy in range(4) if (ox, oy) != (0, 0)]
    arrivals = []
    for i, (src, dst) in enumerate([
        (lrows_hbm, lrows_in), (hidden_hbm, hidden), (queries_hbm, queries),
        (keys_hbm, kvq.at[me.z, me.xh, me.core, 0:128]), (values_hbm, kvq.at[me.z, me.xh, me.core, 128:256]),
        (targets_hbm, targets_in), (gain_hbm, gain_in), (stretch_hbm, stretch),
    ]):
        arrival = pltpu.make_async_copy(src, dst, i_sem.at[i])
        arrival.start()
        arrivals.append(arrival)
    greeted = greet(
        [me.dev(z=me.z_plus(d), core_off=o) for d, o in group1]
        + [me.dev(ox, oy) for ox, oy in group2]
    )
    loads = []
    for j in range(8):
        section = (slice(None), slice(1024 * j, 1024 * j + 1024))
        load = pltpu.make_async_copy(weight_hbm.at[section], weight.at[section], w_sem.at[j])
        load.start()
        loads.append(load)
    out_load = pltpu.make_async_copy(out_hbm, out_weight, o_sem)
    out_load.start()
    started = []

    def go(*args):
        copy = remote(*args)
        started.append(copy)
        return copy

    for arrival in arrivals:
        arrival.wait()
    def drain():
        for copy in started:
            copy.wait_send()
        started.clear()

    lane = lax.broadcasted_iota(jnp.int32, (LPD, ROWS), 1)
    line = lax.broadcasted_iota(jnp.int32, (LPD, ROWS), 0)
    lrows = wide(lrows_in[...]).astype(F32)
    own = jnp.sum(jnp.where(lane == me.c * LPD + line, lrows, 0.0), axis=1, keepdims=True)
    rows_at = lax.broadcasted_iota(jnp.int32, (LPD, 128), 1).astype(F32)
    pick = (own == rows_at).astype(F32).astype(BF16)
    rows[0, me.xh, me.core, me.xl, me.y] = jnp.dot(pick, hidden[...], preferred_element_type=F32).astype(BF16)
    picked_q = jnp.dot(pick, queries[...], preferred_element_type=F32).astype(BF16)
    for head in range(8):
        kvq[me.z, me.xh, me.core, 256 + 8 * head : 264 + 8 * head, :] = picked_q[:, 128 * head : 128 * head + 128]
    greeted()

    def piece(k, at):
        xh, xl, y = at
        return rows.at[pl.ds(2 * k, 2), xh, me.core, xl, y]

    z_copies = {}
    for d in FAR_FIRST[:-1]:
        back = NZ - d
        z_copies[back] = go(
            rows.at[0, me.xh, me.core, me.xl, me.y], rows.at[back, me.xh, me.core, me.xl, me.y],
            z_s.at[d], z_r.at[back], me.dev(z=me.z_plus(d)),
        )
    own_kvq = kvq.at[me.z, me.xh, me.core]
    k_x = go(own_kvq, own_kvq, k_s.at[0], k_r.at[0], me.dev(x_off=2))

    a_copies, f_copies, kf_copies, ring = {}, {}, [], {}

    def spread(k, step):
        order = ORDERS[k]
        for j, at in enumerate(pieces(me, order, step)):
            here = piece(k, at)
            for later in range(step + 1, 4):
                a_copies.setdefault((k, later), []).append(
                    go(
                        here, here, a_s.at[k, later, 2 * step + 2 + j], a_r.at[k, later, 2 * step + 2 + j],
                        partner(me, *order[later]),
                    )
                )
        if step == 3:
            whole = rows.at[pl.ds(2 * k, 2), :, me.core]
            f_copies[k] = [go(whole, whole, f_s.at[k, 0], f_r.at[k, 0], mate)]

    def place_tables():
        spans = jnp.broadcast_to(stretch[...].astype(F32), (8, 64)).astype(BF16)

        def spread_spans(slot, width):
            hot = lax.broadcasted_iota(jnp.int32, (64, width), 0) == slot
            return jnp.dot(spans, hot.astype(F32).astype(BF16), preferred_element_type=F32)[0:1]

        at = lax.broadcasted_iota(jnp.int32, (1, NC * 128), 1)
        base = spread_spans(lax.shift_right_logical(at, 6), NC * 128)
        key_pos[...] = base * 64.0 + (at & 63).astype(F32)
        at = lax.broadcasted_iota(jnp.int32, (1, NC * 64), 1)
        owner = lax.shift_right_logical(at, 6)
        hot = lax.broadcasted_iota(jnp.int32, (ROWS, NC * 64), 0) == owner * LPD + (at & 7)
        local = jnp.dot(
            jnp.broadcast_to(lrows, (8, ROWS)).astype(BF16), hot.astype(F32).astype(BF16), preferred_element_type=F32
        )[0:1]
        first, second = spread_spans(owner * 2, NC * 64), spread_spans(owner * 2 + 1, NC * 64)
        query_pos[...] = jnp.where(local < 64.0, first * 64.0 + local, second * 64.0 + (local - 64.0))
        for t in range(WIDTH // 128):
            gain[:, 128 * t : 128 * t + 128] = gain_in[t : t + 1, :]

    def ring_step(step):
        lo, hi = (0, KVQ) if step < 4 else (0, 160)
        lo2, hi2 = (0, KVQ) if step < 4 else (160, KVQ)
        up, down = me.z_plus(-(step - 1)), me.z_plus(step - 1)
        right = kvq.at[up, :, me.core, lo:hi]
        left = kvq.at[down, :, me.core, lo2:hi2]
        ring[step] = (
            go(right, right, k_s.at[2 * step - 1], k_r.at[2 * step - 1], me.dev(z=me.z_plus(1))),
            go(left, left, k_s.at[2 * step], k_r.at[2 * step], me.dev(z=me.z_plus(-1))),
        )

    def ring_forward(slot, z):
        here = kvq.at[z, :, me.core]
        kf_copies.append(go(here, here, kf_s.at[slot], kf_r.at[slot], mate))

    def ring_wait(step):
        ring[step][0].wait_recv()
        if step < 4:
            ring_forward(2 * step - 1, me.z_plus(-step))
        ring[step][1].wait_recv()
        ring_forward(2 * step if step < 4 else 7, me.z_plus(step))

    def prepare(d, _):
        lines = pl.ds(pl.multiple_of(lax.rem(me.z + d, NZ) * 32, 32), 32)
        square = jnp.zeros((32, 128), F32)
        for v in range(NV):
            cols = slice(1024 * v, 1024 * v + 1024)
            x = rows[d, :, :, v // 4, v % 4].astype(F32).reshape(32, 1024)
            y[lines, cols] = (x * gain[:, cols]).astype(BF16)
            sq = x * x
            for t in range(8):
                square = square + sq[:, 128 * t : 128 * t + 128]
        inv = lax.rsqrt(jnp.sum(square, axis=1, keepdims=True) * (1.0 / WIDTH) + EPS)
        rms_col[lines, :] = jnp.broadcast_to(inv, (32, 128))
        return 0

    place_tables()
    for kind, which in GATHER:
        if kind == "z":
            for d in (2 * which, 2 * which + 1):
                if d:
                    z_copies[d].wait_recv()
            spread(which, -1)
        elif kind == "r":
            if which == 1:
                k_x.wait_recv()
                ring_forward(0, me.z)
            else:
                ring_wait(which - 1)
            ring_step(which)
        elif kind == "p":
            for copy in f_copies[which]:
                copy.wait_recv()
            lax.fori_loop(2 * which, 2 * which + 2, prepare, 0)
        else:
            for copy in a_copies[kind, which]:
                copy.wait_recv()
            spread(kind, which)
    ring_wait(2)
    ring_step(3)

    inv_row = jnp.transpose(rms_col[...])[0:1, :]

    logits[PAD - 48 : PAD, :] = jnp.zeros((48, ROWS), F32)
    for j in range(8):
        loads[j].wait()
        term = lax.dot_general(
            weight[:, 1024 * j : 1024 * j + 1024], y[:, 1024 * j : 1024 * j + 1024],
            (((1,), (1,)), ((), ())), preferred_element_type=F32,
        )
        logits[0:VOC, :] = term if j == 0 else logits[0:VOC, :] + term
        if j == 6:
            ring_wait(3)
            ring_step(4)

    ids = lax.broadcasted_iota(jnp.int32, (PAD, ROWS), 0)
    real = ids < VOC
    first_id = (me.v * NC + me.c) * VOC
    is_target = ((ids + first_id) == wide(targets_in[...])) & real
    value = jnp.where(real, logits[...] * inv_row, FILL)
    logits[...] = value
    top = jnp.max(value, axis=0, keepdims=True)
    raw = jnp.exp(value - top)
    stats = (
        top,
        jnp.sum(raw, axis=0, keepdims=True),
        jnp.sum(raw * value, axis=0, keepdims=True),
        jnp.sum(jnp.where(is_target, value, 0.0), axis=0, keepdims=True),
    )
    packed = jnp.concatenate([piece[:, h : h + 128] for piece in stats for h in (0, 128)], axis=0)
    slot1 = me.z * 2 + me.core
    st1[slot1] = packed
    waits = []
    for i, (d, o) in enumerate(group1):
        waits.append(
            go(st1.at[slot1], st1.at[slot1], s1_s.at[i], s1_r.at[2 * d + o], me.dev(z=me.z_plus(d), core_off=o))
        )
    logits_t[...] = jnp.transpose(logits[...])
    across = lax.broadcasted_iota(jnp.int32, (ROWS, PAD), 1)
    wanted = column(wide(targets_in[...]).astype(F32))[:, 0:1]
    hit_here = ((across + first_id).astype(F32) == wanted) & (across < VOC)
    target_t[...] = hit_here.astype(F32).astype(BF16)
    for copy in waits:
        copy.wait_recv()
    slot2 = (me.xh * 2 + me.xl) * 4 + me.y
    st2[slot2] = merge(st1[...])
    waits = []
    for i, (ox, oy) in enumerate(group2):
        waits.append(go(st2.at[slot2], st2.at[slot2], s2_s.at[i], s2_r.at[4 * ox + oy], me.dev(ox, oy)))
    ring_wait(4)
    for copy in kf_copies:
        copy.wait_recv()

    k_all[...] = kvq[:, :, :, 0:128, :].reshape(NC * 128, HEAD)
    v_all[...] = kvq[:, :, :, 128:256, :].reshape(NC * 128, HEAD)
    q_all[...] = kvq[:, :, :, 256:320, :].reshape(NC * 64, HEAD)
    q_own = kvq[me.z, me.xh, me.core, 256:320, :]
    lane = lax.broadcasted_iota(jnp.int32, (64, NC * 64), 1)
    line = lax.broadcasted_iota(jnp.int32, (64, NC * 64), 0)
    query_col = jnp.sum(jnp.where(lane == me.c * 64 + line, query_pos[...], 0.0), axis=1, keepdims=True)
    scores = lax.dot_general(q_own, k_all[...], (((1,), (1,)), ((), ())), preferred_element_type=F32)
    seen = key_pos[...] <= query_col
    masked = jnp.where(seen, scores * SCALE, FILL)
    top = jnp.max(masked, axis=1, keepdims=True)
    raw = jnp.where(seen, jnp.exp(masked - top), 0.0)
    total = jnp.sum(raw, axis=1, keepdims=True)
    probs[...] = raw / total
    row_log_total = top + jnp.log(total)

    drain()
    for copy in waits:
        copy.wait_recv()
    final = merge(st2[...])
    log_total = wide(final[0:2] + jnp.log(final[2:4]))
    hit = wide(final[6:8])
    grad = jnp.exp(logits_t[...] - column(log_total)[:, 0:1]) - target_t[...].astype(F32)
    grad_t[...] = (GRAD_WEIGHT * grad).astype(BF16)

    def chunk(z, xh, core):
        cols = pl.ds(pl.multiple_of((z * 4 + xh * 2 + core) * 256, 256), 256)
        return jnp.dot(grad_t[:, 0:VOC], weight[:, cols], preferred_element_type=F32).reshape(NV, 32, 256)

    c_copies = {}

    def give(d):
        z = me.z_plus(d)

        def other(xh, _):
            cs[z, xh] = chunk(z, xh, 1 - me.core).astype(BF16)
            return 0

        lax.fori_loop(0, 2, other, 0)
        c_copies[d] = go(cs.at[z], cr.at[z], c_s.at[d], c_r.at[d], mate)

    def keep_own(d):
        z = me.z_plus(d)

        def mine(xh, _):
            acc[z, xh] = chunk(z, xh, me.core)
            return 0

        lax.fori_loop(0, 2, mine, 0)

    sends, recvs = (sb1, sb2, sb3, sb4), (rb1, rb2, rb3, rb4)
    moving = {}

    def at(d, off):
        return (me.z_plus(d), me.xh_off(off[0]), me.v_at(*off))

    def halve(d, part_of, step):
        back = ORDERS[(COLOUR[d] + 2 * part_of) % 4]
        axis, mask = back[3 - step]
        keep, before = offsets(back, 3 - step), offsets(back, 4 - step)
        lines = slice(16 * part_of, 16 * part_of + 16)
        for off in before:
            here = at(d, off) + (lines,)
            if step == 0:
                extra = cr[here].astype(F32)
            else:
                extra = recvs[step - 1][d, part_of, before.index(off)].astype(F32)
            summed = acc[here] + extra
            away = (off[0] ^ mask, off[1]) if axis == "x" else (off[0], off[1] ^ mask)
            if away in keep:
                sends[step][d, part_of, keep.index(away)] = summed.astype(BF16)
            else:
                acc[here] = summed
        moving[d, part_of, step] = go(
            sends[step].at[d, part_of], recvs[step].at[d, part_of],
            x_s.at[d, part_of, step], x_r.at[d, part_of, step], partner(me, axis, mask),
        )

    z_copies = []
    lag = 4
    give(FAR_FIRST[0])
    for i in range(NZ + 4 * lag):
        if i + 1 < NZ:
            give(FAR_FIRST[i + 1])
        if i < NZ:
            d = FAR_FIRST[i]
            keep_own(d)
            c_copies[d].wait_recv()
            for part_of in range(2):
                halve(d, part_of, 0)
        for step in range(1, 5):
            if not 0 <= i - lag * step < NZ:
                continue
            d = FAR_FIRST[i - lag * step]
            for part_of in range(2):
                moving[d, part_of, step - 1].wait_recv()
                if step < 4:
                    halve(d, part_of, step)
                else:
                    lines = slice(16 * part_of, 16 * part_of + 16)
                    zs[d, lines] = (acc[at(d, (0, 0)) + (lines,)] + rb4[d, part_of, 0].astype(F32)).astype(BF16)
            if step < 4:
                continue
            if d:
                z_copies.append(go(zs.at[d], zr.at[me.z], t_s.at[d], t_r.at[d], me.dev(z=me.z_plus(d))))
            else:
                zr[me.z] = zs[d]

    loss[...] = jnp.broadcast_to(jnp.mean(log_total - hit, axis=1, keepdims=True), (8, 128))
    inner_col[...] = column((wide(final[4:6] / final[2:4]) - hit) * (GRAD_WEIGHT / WIDTH))
    k_own = kvq[me.z, me.xh, me.core, 0:128, :]
    v_own = kvq[me.z, me.xh, me.core, 128:256, :]
    s2[...] = lax.dot_general(k_own, q_all[...], (((1,), (1,)), ((), ())), preferred_element_type=F32)
    for copy in z_copies:
        copy.wait_recv()
    normed_grad = jnp.sum(zr[...].astype(F32), axis=0)
    cols = pl.ds(pl.multiple_of(me.c * 256, 256), 256)
    lines = pl.ds(pl.multiple_of(me.v * 32, 32), 32)
    inv = rms_col[lines, 0:1]
    inside = pl.ds(pl.multiple_of(lax.rem(me.c, 4) * 256, 256), 256)
    apart = lax.rem(me.v - me.z + NZ, NZ)
    picked = rows[apart, :, :, lax.div(me.z, 4), lax.rem(me.z, 4), :, inside].astype(F32).reshape(32, 256)
    out = inv * (normed_grad * gain[:, cols] - picked * (inv * inner_col[lines, 0:1]))
    resid[me.v] = out.astype(BF16)
    v_copies = []
    for i, (ox, oy) in enumerate([(o, q) for o in range(2) for q in range(4) if (o, q) != (0, 0)]):
        v_copies.append(go(resid.at[me.v], resid.at[me.v], v_s.at[i], v_r.at[i], me.dev(ox, oy)))
    high = probs[...].astype(BF16)
    low = (probs[...] - high.astype(F32)).astype(BF16)
    attn_out = jnp.dot(high, v_all[...], preferred_element_type=F32) + jnp.dot(
        low, v_all[...], preferred_element_type=F32
    )
    drain()
    for copy in v_copies:
        copy.wait_recv()

    out_load.wait()
    wide_part = lax.dot_general(
        resid[...].reshape(ROWS, 256), out_weight[...], (((1,), (1,)), ((), ())), preferred_element_type=F32
    )
    for h in range(8):
        part[:, :, :, 8 * h : 8 * h + 8, :] = wide_part[:, 128 * h : 128 * h + 128].reshape(NZ, 2, 2, LPD, HEAD)
    pc_copies = {}
    for d in FAR_FIRST:
        z = me.z_plus(d)
        pc[z] = part[z, :, 1 - me.core].astype(BF16)
        pc_copies[d] = go(pc.at[z], pr.at[z], pc_s.at[d], pc_r.at[d], mate)
    x_copies, r_copies = {}, []
    for d in FAR_FIRST:
        z = me.z_plus(d)
        pc_copies[d].wait_recv()
        there = 1 - me.xh
        rs[z] = (part[z, there, me.core] + pr[z, there].astype(F32)).astype(BF16)
        x_copies[d] = go(rs.at[z], rx.at[z], rx_s.at[d], rx_r.at[d], me.dev(x_off=2))
    for d in FAR_FIRST:
        z = me.z_plus(d)
        x_copies[d].wait_recv()
        mine = part[z, me.xh, me.core] + pr[z, me.xh].astype(F32) + rx[z].astype(F32)
        if d:
            rz[z] = mine.astype(BF16)
            r_copies.append(go(rz.at[z], rr.at[me.z], r_s.at[d], r_r.at[d], me.dev(z=z)))
        else:
            rr[me.z] = mine.astype(BF16)
    resid_t[...] = jnp.transpose(resid[...].astype(F32).reshape(ROWS, 256)).astype(BF16)
    drain()
    for copy in r_copies:
        copy.wait_recv()
    grad_own = jnp.sum(rr[...].astype(F32), axis=0).astype(BF16)
    grads[me.z, me.xh, me.core] = grad_own
    own_g, own_e = grads.at[me.z, me.xh, me.core], extras.at[me.z, me.xh, me.core]

    def hand_out(own, send, recv):
        return {d: go(own, own, send.at[d], recv.at[d], me.dev(z=me.z_plus(d))) for d in FAR_FIRST[:-1]}

    g_copies = hand_out(own_g, g_s, g_r)
    delta = jnp.sum(grad_own.astype(F32) * attn_out, axis=1, keepdims=True)
    lane = lax.broadcasted_iota(jnp.int32, (64, 128), 1)
    square_tile[...] = jnp.zeros((128, 128), F32)
    square_tile[0:64, :] = jnp.where(lane == 0, delta, jnp.where(lane == 1, row_log_total, 0.0))
    extras[me.z, me.xh, me.core] = jnp.transpose(square_tile[...])[0:8, :]
    e_copies = hand_out(own_e, e_s, e_r)
    side = me.dev(x_off=2)
    forwards, sides = [], {}

    def hand_on(d, xh, slot):
        here = grads.at[me.z_plus(-d), xh, me.core]
        if not slot:
            sides[d] = go(here, here, gx_s.at[d], gx_r.at[d], side)
        forwards.append(go(here, here, fg_s.at[slot, d], fg_r.at[slot, d], mate))

    hand_on(0, me.xh, 0)
    prob_grad = lax.dot_general(grad_own, v_all[...], (((1,), (1,)), ((), ())), preferred_element_type=F32)
    score_grad = (probs[...] * (prob_grad - delta)).astype(BF16)
    query_grad = jnp.dot(score_grad, k_all[...], preferred_element_type=F32) * SCALE
    for h in range(8):
        dq[:, 128 * h : 128 * h + 128] = query_grad[8 * h : 8 * h + 8, :].astype(BF16)
    for d in NEAR_FIRST[1:]:
        g_copies[d].wait_recv()
        hand_on(d, me.xh, 0)
    for copy in e_copies.values():
        copy.wait_recv()
    line_e = extras.at[:, me.xh, me.core]
    e_side = go(line_e, line_e, ex_s, ex_r, side)
    for d in NEAR_FIRST:
        sides[d].wait_recv()
        hand_on(d, 1 - me.xh, 1)
    e_side.wait_recv()
    all_e = extras.at[:, :, me.core]
    forwards.append(go(all_e, all_e, fe_s, fe_r, mate))
    own_key_pos = key_pos[:, pl.ds(pl.multiple_of(me.c * 128, 128), 128)]
    lane = lax.broadcasted_iota(jnp.int32, (128, 128), 1)
    line = lax.broadcasted_iota(jnp.int32, (128, 128), 0)
    key_col = jnp.sum(jnp.where(lane == line, own_key_pos, 0.0), axis=1, keepdims=True)
    seen2 = key_col <= query_pos[...]
    drain()
    for copy in forwards:
        copy.wait_recv()
    grads_all = grads[...].reshape(NC * 64, HEAD)
    e_all = extras[...].reshape(NC, 8, 128)
    delta_all = jnp.concatenate([e_all[i, 0:1, 0:64] for i in range(NC)], axis=1)
    log_all = jnp.concatenate([e_all[i, 1:2, 0:64] for i in range(NC)], axis=1)
    probs2 = jnp.where(seen2, jnp.exp(s2[...] * SCALE - log_all), 0.0)
    dv[...] = jnp.dot(probs2.astype(BF16), grads_all, preferred_element_type=F32).astype(BF16)
    prob_grad2 = lax.dot_general(v_own, grads_all, (((1,), (1,)), ((), ())), preferred_element_type=F32)
    score_grad2 = (probs2 * (prob_grad2 - delta_all)).astype(BF16)
    dk[...] = (jnp.dot(score_grad2, q_all[...], preferred_element_type=F32) * SCALE).astype(BF16)


def step(*operands):
    vmem = pl.BlockSpec(memory_space=pltpu.VMEM)
    dma = pltpu.SemaphoreType.DMA
    scratch = pltpu.VMEM
    halves = [8, 4, 2, 1]
    return pl.pallas_call(
        step_kernel,
        out_shape=(
            jax.ShapeDtypeStruct((8, 128), F32),
            jax.ShapeDtypeStruct((256, ROWS), BF16),
            jax.ShapeDtypeStruct((LPD, 1024), BF16),
            jax.ShapeDtypeStruct((128, HEAD), BF16),
            jax.ShapeDtypeStruct((128, HEAD), BF16),
        ),
        in_specs=[pl.BlockSpec(memory_space=pl.ANY)] * 10,
        out_specs=(vmem,) * 5,
        scratch_shapes=[
            scratch((VOC, WIDTH), BF16),
            scratch((NZ, 2, 2, 2, 4, LPD, 1024), BF16),
            scratch((ROWS, WIDTH), BF16),
            scratch((NZ, 2, 2, KVQ, HEAD), BF16),
            scratch((PAD, ROWS), F32),
            scratch((ROWS, PAD), F32),
            scratch((ROWS, PAD), BF16),
            scratch((ROWS, PAD), BF16),
            scratch((ROWS, 128), F32),
            scratch((ROWS, 128), F32),
            scratch((16, 8, 128), F32),
            scratch((16, 8, 128), F32),
            scratch((NZ, 2, NV, 32, 256), BF16),
            scratch((NZ, 2, NV, 32, 256), BF16),
            scratch((NZ, 2, NV, 32, 256), F32),
            *[scratch((NZ, 2, n, 16, 256), BF16) for n in halves],
            *[scratch((NZ, 2, n, 16, 256), BF16) for n in halves],
            scratch((NZ, 32, 256), BF16),
            scratch((NZ, 32, 256), BF16),
            scratch((NV, 32, 256), BF16),
            scratch((NC * 128, HEAD), BF16),
            scratch((NC * 128, HEAD), BF16),
            scratch((NC * 64, HEAD), BF16),
            scratch((64, NC * 128), F32),
            scratch((NZ, 2, 2, 64, HEAD), F32),
            *[scratch((NZ, 2, 64, HEAD), BF16)] * 2,
            *[scratch((NZ, 64, HEAD), BF16)] * 4,
            scratch((NZ, 2, 2, 64, HEAD), BF16),
            scratch((NZ, 2, 2, 8, 128), F32),
            scratch((128, 128), F32),
            scratch((128, NC * 64), F32),
            scratch((1, NC * 128), F32),
            scratch((1, NC * 64), F32),
            scratch((1, WIDTH), F32),
            scratch((1024, 256), BF16),
            scratch((128, 1024), BF16),
            scratch((128, 1024), BF16),
            scratch((2, 128), jnp.int32),
            scratch((2, 128), jnp.int32),
            scratch((64, 128), F32),
            scratch((1, 64), jnp.int32),
            dma((8,)), dma, dma((8,)), dma((NZ,)), dma((NZ,)),
            dma((4, 4, 8)), dma((4, 4, 8)), dma((4, 10)), dma((4, 10)),
            dma((9,)), dma((9,)), dma((8,)), dma((8,)),
            dma((16,)), dma((16,)), dma((16,)), dma((16,)), dma((NZ,)), dma((NZ,)),
            dma((NZ, 2, 4)), dma((NZ, 2, 4)), dma((NZ,)), dma((NZ,)), dma((7,)), dma((7,)),
            *[dma((NZ,))] * 12, dma((2, NZ)), dma((2, NZ)), dma, dma, dma, dma,
        ],
        compiler_params=pltpu.CompilerParams(
            collective_id=0, has_side_effects=True, vmem_limit_bytes=61 * 1024 * 1024
        ),
        name="step",
    )(*operands)


def emit_kernel(loss, resid_t, dq, dk, dv, loss_out, resid_out, dq_out, dk_out, dv_out):
    loss_out[0, 0] = loss[0, 0]
    resid_out[...] = resid_t[...]
    dq_out[...] = dq[...]
    dk_out[...] = dk[...]
    dv_out[...] = dv[...]


def emit(loss, *results):
    vmem = pl.BlockSpec(memory_space=pltpu.VMEM)
    return pl.pallas_call(
        emit_kernel,
        out_shape=(jax.ShapeDtypeStruct((1, 1), F32),)
        + tuple(jax.ShapeDtypeStruct(array.shape, array.dtype) for array in results),
        in_specs=[vmem] * 5,
        out_specs=(pl.BlockSpec(memory_space=pltpu.SMEM),) + (vmem,) * 4,
        name="emit",
    )(loss, *results)


def per_device(
    hidden,
    norm_gain,
    head_weight,
    targets,
    loss_rows,
    stretch_of_slot,
    queries,
    key_states,
    attention_values,
    output_weight,
):
    loss, resid_t, dq, dk, dv = step(
        hidden,
        queries,
        key_states,
        attention_values,
        loss_rows.reshape(2, 128),
        targets.reshape(2, 128),
        norm_gain.reshape(64, 128),
        stretch_of_slot.reshape(1, 64),
        output_weight,
        head_weight,
    )
    loss, resid_t, dq, dk, dv = emit(loss, resid_t, dq, dk, dv)
    return (loss[0, 0], dq, dk, dv, resid_t)


def solution(mesh):
    placed = (
        P("ctx", "vocab"),
        P(),
        P(("vocab", "ctx"), None),
        P(),
        P(),
        P(),
        P("ctx", "vocab"),
        P("ctx", "vocab"),
        P("ctx", "vocab"),
        P("vocab", "ctx"),
    )
    return jax.shard_map(
        per_device,
        mesh=mesh,
        in_specs=placed,
        out_specs=(P(), P("ctx", "vocab"), P("ctx", "vocab"), P("ctx", "vocab"), P("ctx", None)),
        check_vma=False,
    )
```
